32 devices in a mesh: dp: 4 (over y, x), seq: 8 (over z, core).
Axes of the slice: x: 2, y: 2, z: 4, core: 2. Of those that a mesh axis runs over, the one named last changes fastest.
Arguments:
- tokens: bfloat16 [4, 16, 16, 4, 512], P('dp', 'seq'), may hold values from -6 to 6
- conv_first: bfloat16 [27, 512, 128], replicated, may hold values from -0.0546875 to 0.0546875
- bias_first: float32 [128], replicated, may hold values from -3 to 3
- conv_second: bfloat16 [27, 128, 384], replicated, may hold values from -0.109375 to 0.109375
- bias_second: float32 [384], replicated, may hold values from -3 to 3
- pixels: bfloat16 [4, 16, 16, 4, 1536], P('dp', None, 'seq'), may hold values from 0 to 1
- mask_index: int32 [4, 57], P('dp'), may hold values from 0 to 63, as said below
Outputs:
- grad_first: float32 [27, 512, 128], P(None, 'seq', 'dp')
- grad_second: float32 [27, 128, 384], P(None, 'seq', 'dp')
The draws below stay inside these ranges and needn't reach their ends.
Inputs may be any that keep to these rules, and one draw needn't show every extreme that they name: `mask_index`: each row holds 57 distinct positions of the 16 x 4 token grid.
All inputs are finite; a program needn't handle non-finite values.
Results may differ from the reference program's by a relative error of at most 0.003.
Values may be sent and summed in bfloat16 or wider, within the bound.
A program may use at most 128 MiB of HBM per device.

```python
from functools import partial
import jax
import jax.numpy as jnp
from jax import lax

D = 512
C1 = 128
CO = 384
T_SIZE = 16
W = 4
H = 16
CLIPS = 4
MASKED = 57


def draw_mask_index(key, part):
    clip_keys = jax.random.split(jax.random.fold_in(key, 17), CLIPS)
    orders = jax.vmap(lambda one_key: jax.random.permutation(one_key, H * W))(clip_keys)
    return orders[:, :MASKED].astype(jnp.int32)


def level_of(own_key, shape, cuts, low, high):
    loudness, own = 1.0, jax.random.fold_in(own_key, 6)
    for position, blocks in cuts:
        heights = jnp.exp(jax.random.uniform(jax.random.fold_in(own, position), (blocks,), jnp.float32, low / len(cuts), high / len(cuts)))
        loudness = loudness * jnp.repeat(heights, shape[position] // blocks).reshape([-1 if axis == position else 1 for axis in range(len(shape))])
    return loudness


def gaussian(own_key, extent, scale, limit, cuts=(), kind=jnp.bfloat16):
    level = level_of(own_key, extent, cuts, -0.22, 0.18) if cuts else 1.0
    drawn = jax.random.normal(own_key, extent, jnp.float32) * scale * level
    return jnp.minimum(jnp.maximum(drawn, -limit), limit).astype(kind)


def setup_inputs(seed: int = 0) -> dict:
    key_list = jax.random.split(jax.random.key(seed), 8)
    return {
        "tokens": gaussian(key_list[0], (CLIPS, T_SIZE, H, W, D), 1.0, 6.0, ((0, 4), (1, 8))),
        "conv_first": gaussian(key_list[1], (27, D, C1), (27 * D) ** -0.5, 0.0546875),
        "bias_first": gaussian(key_list[2], (C1,), 0.5, 3.0, (), jnp.float32),
        "conv_second": gaussian(key_list[3], (27, C1, CO), (27 * C1) ** -0.5, 0.109375),
        "bias_second": gaussian(key_list[4], (CO,), 0.5, 3.0, (), jnp.float32),
        "pixels": jnp.clip(1.0 * jax.random.uniform(key_list[5], (CLIPS, T_SIZE, H, W, 4 * CO), jnp.float32) ** level_of(key_list[5], (CLIPS, T_SIZE, H, W, 4 * CO), ((0, 4), (2, 8)), -0.2, 0.2), 0.0, 1.0).astype(jnp.bfloat16),
        "mask_index": draw_mask_index(jax.random.fold_in(key_list[7], 71), 0),
    }


def shifts_of(tap_index):
    return (tap_index // 9, tap_index // 3 % 3, tap_index % 3)

def pad_full(field):
    return jnp.pad(field, ((1, 1), (1, 1), (1, 1), (0, 0)))

def conv_taps(padded, weight):
    frames = padded.shape[0] - 2
    rows = padded.shape[1] - 2
    cols = padded.shape[2] - 2
    summed = jnp.zeros((frames * rows * cols, weight.shape[2]), jnp.float32)
    for tap_index in range(27):
        shift_time, shift_row, shift_col = shifts_of(tap_index)
        window = padded[shift_time:shift_time + frames, shift_row:shift_row + rows, shift_col:shift_col + cols]
        summed = summed + jnp.dot(window.reshape(-1, padded.shape[3]), weight[tap_index], preferred_element_type=jnp.float32)
    return summed.reshape(frames, rows, cols, weight.shape[2])

def tap_grads(padded, cotangent):
    frames, rows, cols, width = cotangent.shape
    flat = cotangent.reshape(-1, width)
    result = []
    for tap_index in range(27):
        shift_time, shift_row, shift_col = shifts_of(tap_index)
        window = padded[shift_time:shift_time + frames, shift_row:shift_row + rows, shift_col:shift_col + cols]
        result.append(lax.dot_general(window.reshape(-1, padded.shape[3]), flat, (((0,), (0,)), ((), ())), preferred_element_type=jnp.float32))
    return jnp.stack(result)

def conv_back(padded, weight):
    frames = padded.shape[0] - 2
    rows = padded.shape[1] - 2
    cols = padded.shape[2] - 2
    summed = jnp.zeros((frames * rows * cols, weight.shape[1]), jnp.float32)
    for tap_index in range(27):
        shift_time, shift_row, shift_col = shifts_of(tap_index)
        window = padded[2 - shift_time:2 - shift_time + frames, 2 - shift_row:2 - shift_row + rows, 2 - shift_col:2 - shift_col + cols]
        summed = summed + lax.dot_general(window.reshape(-1, padded.shape[3]), weight[tap_index], (((1,), (1,)), ((), ())), preferred_element_type=jnp.float32)
    return summed.reshape(frames, rows, cols, weight.shape[1])

def reference(tokens, conv_first, bias_first, conv_second, bias_second, pixels, mask_index):
    gelu_tanh = partial(jax.nn.gelu, approximate=True)

    def per_clip(carry, inputs):
        clip_tokens, clip_pixels, clip_index = inputs
        frames, rows, cols, width = clip_tokens.shape
        tokens_padded = pad_full(clip_tokens)
        zsum = conv_taps(tokens_padded, conv_first) + bias_first
        hidden = gelu_tanh(zsum).astype(jnp.bfloat16)
        upsampled = jnp.repeat(jnp.repeat(hidden, 2, axis=1), 2, axis=2)
        up_padded = pad_full(upsampled)
        predict = conv_taps(up_padded, conv_second) + bias_second
        values = predict.shape[3]
        pix = clip_pixels.astype(jnp.float32)
        center = pix - lax.optimization_barrier(jnp.mean(pix, axis=-1, keepdims=True))
        spread = lax.optimization_barrier(jnp.mean(center * center, axis=-1, keepdims=True))
        normed = center * lax.rsqrt(spread + 1e-06)
        normed = normed.reshape(frames, rows, cols, 2, 2, values).transpose(0, 1, 3, 2, 4, 5).reshape(frames, 2 * rows, 2 * cols, values)
        positions = jnp.arange(rows * cols, dtype=jnp.int32)
        hits = lax.optimization_barrier(jnp.sum((positions[:, None] == clip_index[None, :]).astype(jnp.float32), axis=1)).reshape(rows, cols)
        cell_mask = jnp.repeat(jnp.repeat(hits, 2, axis=0), 2, axis=1)
        cotangent = (2.0 / (4 * values) * cell_mask[None, :, :, None] * (predict - normed)).astype(jnp.bfloat16)
        grad_second = tap_grads(up_padded, cotangent)
        grad_up = conv_back(pad_full(cotangent), conv_second)
        grad_hidden = grad_up.reshape(frames, rows, 2, cols, 2, grad_up.shape[3]).sum(axis=(2, 4))
        grad_z = jax.vjp(gelu_tanh, zsum)[1](grad_hidden)[0].astype(jnp.bfloat16)
        grad_first = tap_grads(tokens_padded, grad_z)
        return ((carry[0] + grad_first, carry[1] + grad_second), None)
    start = (jnp.zeros(conv_first.shape, jnp.float32), jnp.zeros(conv_second.shape, jnp.float32))
    final, unused = lax.scan(per_clip, start, (tokens, pixels, mask_index))
    return (final[0], final[1])
```

```python
import jax
import jax.numpy as jnp
from jax import lax
from jax.experimental import pallas as pl
from jax.experimental.pallas import tpu as pltpu
from jax.sharding import PartitionSpec as P

F32 = jnp.float32
BF16 = jnp.bfloat16
NT = (((1,), (1,)), ((), ()))
GELU_ROOT = 0.7978845608028654
GELU_CUBE = 0.044715


def floor_half(v):
    return v // 2 if v >= 0 else -1


def make_kernel(dims):
    ndp, nseq, frames, tf, rows, cols, width, mid, values = dims
    n = tf * cols * rows
    plane = cols * rows
    dblk = width // nseq
    cblk = mid // ndp
    vblk = values // ndp
    mblk = mid // nseq
    ndev = ndp * nseq
    clip_lanes = nseq * n

    def kernel(tok, w1_hbm, b1, w2_hbm, b2, pix, perm, colv, lanev, lanes_n, o1, o2,
               w1, w2, xbuf, xall, thalo, pxall, tfield, im1, hsend, hhalo, hfield, im2,
               psend, phalo, csend, call_, htsend, htall, rsend, rall, gsend, gall, acc,
               wsem, th_s, th_r, px_s, px_r, x_s, x_r, hh_s, hh_r, ph_s, ph_r,
               c_s, c_r, ht_s, ht_r, r_s, r_r, g_s, g_r):
        dp = lax.axis_index("dp")
        seq = lax.axis_index("seq")
        me = dp * nseq + seq
        nxt = lax.rem(seq + 1, nseq)
        prv = lax.rem(seq + nseq - 1, nseq)

        def remote(src, dst, ss, rs, d, s):
            return pltpu.make_async_remote_copy(
                src_ref=src, dst_ref=dst, send_sem=ss, recv_sem=rs,
                device_id=(d, s), device_id_type=pl.DeviceIdType.MESH)

        cp1 = pltpu.make_async_copy(w1_hbm, w1, wsem.at[0])
        cp2 = pltpu.make_async_copy(w2_hbm, w2, wsem.at[1])
        cp1.start()
        cp2.start()

        barrier = pltpu.get_barrier_semaphore()

        def greet(o, c):
            t = lax.rem(me + o, ndev)
            pl.semaphore_signal(barrier, inc=1, device_id=(t // nseq, lax.rem(t, nseq)),
                                device_id_type=pl.DeviceIdType.MESH)
            return c

        lax.fori_loop(1, ndev, greet, 0)

        flat = tok[...].reshape(n, width).astype(F32)
        xt = flat.T
        for s in range(nseq):
            xbuf[s] = xt[s * dblk:(s + 1) * dblk].astype(BF16)
        pl.semaphore_wait(barrier, ndev - 1)

        def halo(first, last, dst, ss, rs):
            return (remote(last, dst.at[0], ss.at[0], rs.at[0], dp, nxt),
                    remote(first, dst.at[1], ss.at[1], rs.at[1], dp, prv))

        th = halo(tok.at[0], tok.at[tf - 1], thalo, th_s, th_r)
        for c in th:
            c.start()

        def px_copy(o):
            s = lax.rem(seq + o, nseq)
            return remote(pix.at[s], pxall.at[seq], px_s.at[o], px_r.at[seq], dp, s)

        def px_arrival(o):
            s = lax.rem(seq + nseq - o, nseq)
            return remote(pix.at[s], pxall.at[s], px_s.at[o], px_r.at[s], dp, s)

        def x_copy(o):
            t = lax.rem(me + o, ndev)
            s = lax.rem(t, nseq)
            return remote(xbuf.at[s], xall.at[me], x_s.at[o], x_r.at[me], t // nseq, s)

        def x_arrival(o):
            t = lax.rem(me + ndev - o, ndev)
            s = lax.rem(t, nseq)
            return remote(xbuf.at[s], xall.at[t], x_s.at[o], x_r.at[t], t // nseq, s)

        def c_pair(o):
            d = lax.rem(dp + o, ndp)
            return (remote(csend.at[d], call_.at[dp], c_s.at[o], c_r.at[dp], d, seq),
                    remote(htsend, htall.at[dp], ht_s.at[o], ht_r.at[dp], d, seq))

        def c_arrival(o):
            d = lax.rem(dp + ndp - o, ndp)
            return (remote(csend.at[d], call_.at[d], c_s.at[o], c_r.at[d], d, seq),
                    remote(htsend, htall.at[d], ht_s.at[o], ht_r.at[d], d, seq))

        def r_copy(o):
            s = lax.rem(seq + o, nseq)
            return remote(rsend.at[s], rall.at[seq], r_s.at[o], r_r.at[seq], dp, s)

        def r_arrival(o):
            s = lax.rem(seq + nseq - o, nseq)
            return remote(rsend.at[s], rall.at[s], r_s.at[o], r_r.at[s], dp, s)

        def g_copy(o):
            t = lax.rem(me + o, ndev)
            d = t // nseq
            return remote(gsend.at[d], gall.at[me], g_s.at[o], g_r.at[me], d, lax.rem(t, nseq))

        def g_arrival(o):
            t = lax.rem(me + ndev - o, ndev)
            d = t // nseq
            return remote(gsend.at[d], gall.at[t], g_s.at[o], g_r.at[t], d, lax.rem(t, nseq))

        def each(count, act):
            def body(o, c):
                act(o)
                return c
            lax.fori_loop(1, count, body, 0)

        def start_all(count, copy):
            each(count, lambda o: copy(o).start())

        def finish(count, copy, arrival):
            each(count, lambda o: copy(o).wait_send())
            each(count, lambda o: arrival(o).wait_recv())

        start_all(nseq, px_copy)
        start_all(ndev, x_copy)
        xall[me] = xbuf[seq]
        pxall[seq] = pix[seq]

        scale = colv[:, 0:1]
        h_low, h_high = colv[:, 1:2], colv[:, 2:3]
        w_low, w_high = colv[:, 3:4], colv[:, 4:5]

        def row_shift(v, d):
            m = v.shape[0]
            if d == 0:
                return v
            rolled = pltpu.roll(v, 1 if d < 0 else m - 1, axis=0)
            return rolled * (h_low if d < 0 else h_high)[:m]

        def col_shift(v, d):
            m = v.shape[0]
            if d == 0:
                return v
            rolled = pltpu.roll(v, rows if d < 0 else m - rows, axis=0)
            return rolled * (w_low if d < 0 else w_high)[:m]

        def place(field, frame, v, count):
            for d in (-1, 0, 1):
                field[d + 1, frame:frame + count, 1:cols + 1] = (
                    row_shift(v, d).astype(BF16).reshape(count, cols, rows, v.shape[1]))

        def edges(field):
            zero = jnp.zeros((3, tf + 2, 1, rows, field.shape[4]), BF16)
            field[:, :, 0:1] = zero
            field[:, :, cols + 1:cols + 2] = zero

        first = jnp.where(seq > 0, 1.0, 0.0).astype(F32)
        final = jnp.where(seq < nseq - 1, 1.0, 0.0).astype(F32)

        edges(tfield)
        edges(hfield)
        place(tfield, 1, flat, tf)
        for c in th:
            c.wait()
        place(tfield, 0, thalo[0].reshape(plane, width).astype(F32) * first, 1)
        place(tfield, tf + 1, thalo[1].reshape(plane, width).astype(F32) * final, 1)
        for k in range(27):
            a, b, c = k // 9, k // 3 % 3, k % 3
            im1[:, k * width:(k + 1) * width] = (
                tfield[b, a:a + tf, c:c + cols].reshape(n, width))
        cp1.wait()
        z = jnp.dot(im1[...], w1[...], preferred_element_type=F32) + b1[...]
        th_ = jnp.tanh(GELU_ROOT * (z + GELU_CUBE * z * z * z))
        slope = 0.5 * (1.0 + th_) + 0.5 * z * (1.0 - th_ * th_) * GELU_ROOT * (
            1.0 + 3.0 * GELU_CUBE * z * z)
        hid = (0.5 * z * (1.0 + th_)).astype(BF16)
        hsend[...] = hid.reshape(tf, cols, rows, mid)
        hh = halo(hsend.at[0], hsend.at[tf - 1], hhalo, hh_s, hh_r)
        for c in hh:
            c.start()
        hid_f = hid.astype(F32)
        place(hfield, 1, hid_f, tf)

        finish(nseq, px_copy, px_arrival)
        pix_rows = pxall[...].astype(F32).reshape(n, 4 * values).astype(BF16)
        px = jnp.dot(perm[...], pix_rows, preferred_element_type=F32)
        center = px - jnp.mean(px, axis=-1, keepdims=True)
        spread = jnp.mean(center * center, axis=-1, keepdims=True)
        normed = center * lax.rsqrt(spread + 1e-06)

        for c in hh:
            c.wait()
        before = hhalo[0].reshape(plane, mid).astype(F32) * first
        after = hhalo[1].reshape(plane, mid).astype(F32) * final
        place(hfield, 0, before, 1)
        place(hfield, tf + 1, after, 1)

        for ij in range(4):
            i, j = ij // 2, ij % 2
            for k in range(27):
                a, b, c = k // 9, k // 3 % 3, k % 3
                dh, dw = floor_half(i + b - 1), floor_half(j + c - 1)
                im2[ij * n:(ij + 1) * n, k * mid:(k + 1) * mid] = (
                    hfield[dh + 1, a:a + tf, dw + 1:dw + 1 + cols].reshape(n, mid))
        cp2.wait()
        predict = jnp.dot(im2[...], w2[...], preferred_element_type=F32) + b2[...]
        cots = []
        for ij in range(4):
            cot = (scale * (predict[ij * n:(ij + 1) * n]
                            - normed[:, ij * values:(ij + 1) * values])).astype(BF16).astype(F32)
            cots.append(cot)
            turned = cot.T
            for d in range(ndp):
                csend[d, ij] = turned[d * vblk:(d + 1) * vblk].astype(BF16)
        time_line = jnp.concatenate([before, hid_f, after], axis=0)
        for a in range(3):
            htsend[a * mid:(a + 1) * mid] = (
                time_line[a * plane:a * plane + n].T.astype(BF16))
        each(ndp, lambda o: [c.start() for c in c_pair(o)])
        call_[dp] = csend[dp]
        htall[dp] = htsend[...]

        def pair_sums(low, high, shift):
            return (high + shift(low, 1), low + high, shift(high, -1) + low)

        def cell_sums(parts, rshift, cshift):
            by_col = [pair_sums(parts[j], parts[2 + j], rshift) for j in range(2)]
            return [s for b in range(3)
                    for s in pair_sums(by_col[0][b], by_col[1][b], cshift)]

        sums = [s.astype(BF16) for s in cell_sums(cots, row_shift, col_shift)]
        backs = []
        for a in range(3):
            total = jnp.zeros((n, mid), F32)
            for bc in range(9):
                k = a * 9 + bc
                total = total + lax.dot_general(
                    sums[bc], w2[k * mid:(k + 1) * mid], NT, preferred_element_type=F32)
            backs.append(total)
        psend[0] = backs[2][n - plane:]
        psend[1] = backs[0][:plane]
        ph = halo(psend.at[1], psend.at[0], phalo, ph_s, ph_r)
        for c in ph:
            c.start()
        for c in ph:
            c.wait()
        from_prev, from_next = phalo[0] * first, phalo[1] * final
        if tf > 1:
            late = jnp.concatenate([from_prev, backs[2][:n - plane]], axis=0)
            early = jnp.concatenate([backs[0][plane:], from_next], axis=0)
        else:
            late, early = from_prev, from_next
        grad_z = ((backs[1] + late + early) * slope).astype(BF16).astype(F32).T
        for d in range(ndp):
            gsend[d] = grad_z[d * cblk:(d + 1) * cblk].astype(BF16)
        start_all(ndev, g_copy)
        gall[me] = gsend[dp]

        each(ndp, lambda o: [c.wait_send() for c in c_pair(o)])
        each(ndp, lambda o: [c.wait_recv() for c in c_arrival(o)])

        def lane_row(v, d):
            rolled = pltpu.roll(v, 1 if d < 0 else n - 1, axis=1)
            return rolled * (lanes_n[0:1] if d < 0 else lanes_n[1:2])

        def lane_col(v, d):
            rolled = pltpu.roll(v, rows if d < 0 else n - rows, axis=1)
            return rolled * (lanes_n[2:3] if d < 0 else lanes_n[3:4])

        acc[...] = jnp.zeros_like(acc)

        def one_clip(q, carry):
            parts = [call_[q, ij].astype(F32) for ij in range(4)]
            stack = jnp.concatenate(cell_sums(parts, lane_row, lane_col), axis=0).astype(BF16)
            acc[...] += lax.dot_general(htall[q], stack, NT, preferred_element_type=F32)
            return carry

        lax.fori_loop(0, ndp, one_clip, 0)
        for s in range(nseq):
            for a in range(3):
                lo = a * mid + s * mblk
                rsend[s, a] = acc[lo:lo + mblk].astype(BF16)
        start_all(nseq, r_copy)
        rall[seq] = rsend[seq]

        finish(ndev, x_copy, x_arrival)
        finish(ndev, g_copy, g_arrival)
        o1[...] = jnp.zeros_like(o1)

        def one_first(q, carry):
            base = q * nseq
            g = jnp.concatenate([gall[base + s].astype(F32) for s in range(nseq)], axis=1)
            x = jnp.concatenate([xall[base + s] for s in range(nseq)], axis=1)
            pieces = []
            by_row = []
            for b in range(3):
                d = b - 1
                if d == 0:
                    by_row.append(g)
                else:
                    m = pltpu.roll(g, d % clip_lanes, axis=1)
                    by_row.append(m * (lanev[0:1] if d > 0 else lanev[1:2]))
            grid = {}
            for b in range(3):
                for c in range(3):
                    d = c - 1
                    v = by_row[b]
                    if d != 0:
                        v = pltpu.roll(v, (d * rows) % clip_lanes, axis=1)
                        v = v * (lanev[2:3] if d > 0 else lanev[3:4])
                    grid[b, c] = v
            for a in range(3):
                for b in range(3):
                    for c in range(3):
                        d = a - 1
                        v = grid[b, c]
                        if d != 0:
                            v = pltpu.roll(v, (d * plane) % clip_lanes, axis=1)
                            v = v * (lanev[4:5] if d > 0 else lanev[5:6])
                        pieces.append(v)
            stack = jnp.concatenate(pieces, axis=0).astype(BF16)
            o1[...] += lax.dot_general(stack, x, NT, preferred_element_type=F32)
            return carry

        lax.fori_loop(0, ndp, one_first, 0)

        finish(nseq, r_copy, r_arrival)
        total = rall[0].astype(F32)
        for s in range(1, nseq):
            total = total + rall[s].astype(F32)
        o2[...] = total

    return kernel


def per_device(tokens, conv_first, bias_first, conv_second, bias_second, pixels, mask_index):
    ndp, nseq = lax.axis_size("dp"), lax.axis_size("seq")
    tf, rows, cols, width = tokens.shape[1:]
    frames = tf * nseq
    mid, values = conv_second.shape[1], conv_second.shape[2]
    n = tf * rows * cols
    hb = rows // nseq
    dims = (ndp, nseq, frames, tf, rows, cols, width, mid, values)
    plane = rows * cols
    dblk, cblk, vblk, mblk = width // nseq, mid // ndp, values // ndp, mid // nseq
    ndev = ndp * nseq

    tok = tokens[0].transpose(0, 2, 1, 3)
    pix = pixels[0].reshape(nseq, tf * hb * cols, 4 * values)
    idx = jnp.arange(n, dtype=jnp.int32)
    t_of, w_of, h_of = idx // plane, idx // rows % cols, idx % rows
    source = (h_of // hb) * (tf * hb * cols) + t_of * (hb * cols) + (h_of % hb) * cols + w_of
    perm = (source[:, None] == idx[None, :]).astype(BF16)
    position = h_of * cols + w_of
    hits = jnp.sum((position[:, None] == mask_index[0][None, :]).astype(F32), axis=1)
    colv = jnp.stack([2.0 / (4 * values) * hits, h_of > 0, h_of < rows - 1,
                      w_of > 0, w_of < cols - 1], axis=1).astype(F32)
    lanes_n = jnp.stack([h_of > 0, h_of < rows - 1, w_of > 0, w_of < cols - 1]).astype(F32)
    lid = jnp.arange(frames * plane, dtype=jnp.int32)
    tl, wl, hl = lid // plane, lid // rows % cols, lid % rows
    lanev = jnp.stack([hl > 0, hl < rows - 1, wl > 0, wl < cols - 1,
                       tl > 0, tl < frames - 1]).astype(F32)

    vm = pl.BlockSpec(memory_space=pltpu.VMEM)
    hbm = pl.BlockSpec(memory_space=pl.ANY)

    def dma(k):
        return pltpu.SemaphoreType.DMA((k,))

    scratch = [
        pltpu.VMEM((27 * width, mid), BF16),
        pltpu.VMEM((27 * mid, values), BF16),
        pltpu.VMEM((nseq, dblk, n), BF16),
        pltpu.VMEM((ndev, dblk, n), BF16),
        pltpu.VMEM((2, cols, rows, width), BF16),
        pltpu.VMEM(pix.shape, BF16),
        pltpu.VMEM((3, tf + 2, cols + 2, rows, width), BF16),
        pltpu.VMEM((n, 27 * width), BF16),
        pltpu.VMEM((tf, cols, rows, mid), BF16),
        pltpu.VMEM((2, cols, rows, mid), BF16),
        pltpu.VMEM((3, tf + 2, cols + 2, rows, mid), BF16),
        pltpu.VMEM((4 * n, 27 * mid), BF16),
        pltpu.VMEM((2, plane, mid), F32),
        pltpu.VMEM((2, plane, mid), F32),
        pltpu.VMEM((ndp, 4, vblk, n), BF16),
        pltpu.VMEM((ndp, 4, vblk, n), BF16),
        pltpu.VMEM((3 * mid, n), BF16),
        pltpu.VMEM((ndp, 3 * mid, n), BF16),
        pltpu.VMEM((nseq, 3, mblk, 9 * vblk), BF16),
        pltpu.VMEM((nseq, 3, mblk, 9 * vblk), BF16),
        pltpu.VMEM((ndp, cblk, n), BF16),
        pltpu.VMEM((ndev, cblk, n), BF16),
        pltpu.VMEM((3 * mid, 9 * vblk), F32),
        dma(2), dma(2), dma(2), dma(nseq), dma(nseq), dma(ndev), dma(ndev),
        dma(2), dma(2), dma(2), dma(2), dma(ndp), dma(ndp), dma(ndp), dma(ndp),
        dma(nseq), dma(nseq), dma(ndev), dma(ndev),
    ]
    first, second = pl.pallas_call(
        make_kernel(dims),
        out_shape=(jax.ShapeDtypeStruct((27 * cblk, dblk), F32),
                   jax.ShapeDtypeStruct((3, mblk, 9 * vblk), F32)),
        in_specs=[vm, hbm, vm, hbm, vm, vm, vm, vm, vm, vm],
        out_specs=(vm, vm),
        scratch_shapes=scratch,
        compiler_params=pltpu.CompilerParams(
            collective_id=0, has_side_effects=True, vmem_limit_bytes=60 * 1024 * 1024),
        name="step",
    )(tok, conv_first.reshape(27 * width, mid), bias_first.reshape(1, mid),
      conv_second.reshape(27 * mid, values), bias_second.reshape(1, values),
      pix, perm, colv, lanev, lanes_n)
    first = first.reshape(27, cblk, dblk).transpose(0, 2, 1)
    second = second.reshape(3, mblk, 9, vblk).transpose(0, 2, 1, 3).reshape(27, mblk, vblk)
    return (first, second)


def solution(mesh):
    return jax.shard_map(
        per_device,
        mesh=mesh,
        in_specs=(
            P("dp", "seq", None, None, None),
            P(),
            P(),
            P(),
            P(),
            P("dp", None, "seq", None, None),
            P("dp", None),
        ),
        out_specs=(P(None, "seq", "dp"), P(None, "seq", "dp")),
        check_vma=False,
    )
```

```python
import jax
import jax.numpy as jnp
import numpy as np
from jax import lax
from jax.experimental import pallas as pl
from jax.experimental.pallas import tpu as pltpu
from jax.sharding import PartitionSpec as P

F32 = jnp.float32
BF16 = jnp.bfloat16
NT = (((1,), (1,)), ((), ()))
GELU_ROOT = 0.7978845608028654
GELU_CUBE = 0.044715


def floor_half(v):
    return v // 2 if v >= 0 else -1


def make_kernel(dims):
    ndp, nseq, frames, tf, rows, cols, width, mid, values = dims
    n = tf * cols * rows
    plane = cols * rows
    dblk = width // nseq
    cblk = mid // ndp
    vblk = values // ndp
    mblk = mid // nseq
    ndev = ndp * nseq
    clip_lanes = nseq * n

    def kernel(tok, w1_hbm, b1, w2_hbm, b2, pix, marks, place_of, tperm, perm, colv, lanev,
               lanes_n, o1, o2,
               w1, w2, xbuf, xall, thalo, pxall, tfield, im1, hsend, hhalo, hfield, im2,
               psend, phalo, csend, call_, htsend, htall, rsend, rall, gsend, gall, acc,
               wsem, th_s, th_r, px_s, px_r, x_s, x_r, hh_s, hh_r, ph_s, ph_r,
               c_s, c_r, ht_s, ht_r, r_s, r_r, g_s, g_r):
        dp = lax.axis_index("dp")
        seq = lax.axis_index("seq")
        me = dp * nseq + seq
        nxt = lax.rem(seq + 1, nseq)
        prv = lax.rem(seq + nseq - 1, nseq)

        def remote(src, dst, ss, rs, d, s):
            return pltpu.make_async_remote_copy(
                src_ref=src, dst_ref=dst, send_sem=ss, recv_sem=rs,
                device_id=(d, s), device_id_type=pl.DeviceIdType.MESH)

        cp1 = pltpu.make_async_copy(w1_hbm, w1, wsem.at[0])
        cp2 = pltpu.make_async_copy(w2_hbm, w2, wsem.at[1])
        cp1.start()
        cp2.start()

        barrier = pltpu.get_barrier_semaphore()

        def greet(o, c):
            t = lax.rem(me + o, ndev)
            pl.semaphore_signal(barrier, inc=1, device_id=(t // nseq, lax.rem(t, nseq)),
                                device_id_type=pl.DeviceIdType.MESH)
            return c

        lax.fori_loop(1, ndev, greet, 0)

        def ordered(frame):
            raw = frame.astype(F32).reshape(plane, width).astype(BF16)
            return jnp.dot(tperm[...], raw, preferred_element_type=F32)

        flat = jnp.concatenate([ordered(tok[t]) for t in range(tf)], axis=0)
        xt = flat.T
        for s in range(nseq):
            xbuf[s] = xt[s * dblk:(s + 1) * dblk].astype(BF16)
        pl.semaphore_wait(barrier, ndev - 1)

        def halo(first, last, dst, ss, rs):
            return (remote(last, dst.at[0], ss.at[0], rs.at[0], dp, nxt),
                    remote(first, dst.at[1], ss.at[1], rs.at[1], dp, prv))

        th = halo(tok.at[0], tok.at[tf - 1], thalo, th_s, th_r)
        for c in th:
            c.start()

        def px_copy(o):
            s = lax.rem(seq + o, nseq)
            return remote(pix.at[pl.ds(s * tf, tf)], pxall.at[seq], px_s.at[o], px_r.at[seq],
                          dp, s)

        def px_arrival(o):
            s = lax.rem(seq + nseq - o, nseq)
            return remote(pix.at[pl.ds(s * tf, tf)], pxall.at[s], px_s.at[o], px_r.at[s], dp, s)

        def x_copy(o):
            t = lax.rem(me + o, ndev)
            s = lax.rem(t, nseq)
            return remote(xbuf.at[s], xall.at[me], x_s.at[o], x_r.at[me], t // nseq, s)

        def x_arrival(o):
            t = lax.rem(me + ndev - o, ndev)
            s = lax.rem(t, nseq)
            return remote(xbuf.at[s], xall.at[t], x_s.at[o], x_r.at[t], t // nseq, s)

        def c_pair(o):
            d = lax.rem(dp + o, ndp)
            return (remote(csend.at[d], call_.at[dp], c_s.at[o], c_r.at[dp], d, seq),
                    remote(htsend, htall.at[dp], ht_s.at[o], ht_r.at[dp], d, seq))

        def c_arrival(o):
            d = lax.rem(dp + ndp - o, ndp)
            return (remote(csend.at[d], call_.at[d], c_s.at[o], c_r.at[d], d, seq),
                    remote(htsend, htall.at[d], ht_s.at[o], ht_r.at[d], d, seq))

        def r_copy(o):
            s = lax.rem(seq + o, nseq)
            return remote(rsend.at[s], rall.at[seq], r_s.at[o], r_r.at[seq], dp, s)

        def r_arrival(o):
            s = lax.rem(seq + nseq - o, nseq)
            return remote(rsend.at[s], rall.at[s], r_s.at[o], r_r.at[s], dp, s)

        def g_copy(o):
            t = lax.rem(me + o, ndev)
            d = t // nseq
            return remote(gsend.at[d], gall.at[me], g_s.at[o], g_r.at[me], d, lax.rem(t, nseq))

        def g_arrival(o):
            t = lax.rem(me + ndev - o, ndev)
            d = t // nseq
            return remote(gsend.at[d], gall.at[t], g_s.at[o], g_r.at[t], d, lax.rem(t, nseq))

        def each(count, act):
            def body(o, c):
                act(o)
                return c
            lax.fori_loop(1, count, body, 0)

        def start_all(count, copy):
            each(count, lambda o: copy(o).start())

        def finish(count, copy, arrival):
            each(count, lambda o: copy(o).wait_send())
            each(count, lambda o: arrival(o).wait_recv())

        start_all(nseq, px_copy)
        start_all(ndev, x_copy)
        xall[me] = xbuf[seq]
        own = pltpu.make_async_copy(pix.at[pl.ds(seq * tf, tf)], pxall.at[seq], wsem.at[2])
        own.start()

        matches = (place_of[...] == marks[...]).astype(F32)
        scale = 2.0 / (4 * values) * jnp.sum(matches, axis=1, keepdims=True)
        h_low, h_high = colv[:, 1:2], colv[:, 2:3]
        w_low, w_high = colv[:, 3:4], colv[:, 4:5]

        def row_shift(v, d):
            m = v.shape[0]
            if d == 0:
                return v
            rolled = pltpu.roll(v, 1 if d < 0 else m - 1, axis=0)
            return rolled * (h_low if d < 0 else h_high)[:m]

        def col_shift(v, d):
            m = v.shape[0]
            if d == 0:
                return v
            rolled = pltpu.roll(v, rows if d < 0 else m - rows, axis=0)
            return rolled * (w_low if d < 0 else w_high)[:m]

        def place(field, frame, v, count):
            for d in (-1, 0, 1):
                field[d + 1, frame:frame + count, 1:cols + 1] = (
                    row_shift(v, d).astype(BF16).reshape(count, cols, rows, v.shape[1]))

        def edges(field):
            zero = jnp.zeros((3, tf + 2, 1, rows, field.shape[4]), BF16)
            field[:, :, 0:1] = zero
            field[:, :, cols + 1:cols + 2] = zero

        first = jnp.where(seq > 0, 1.0, 0.0).astype(F32)
        final = jnp.where(seq < nseq - 1, 1.0, 0.0).astype(F32)

        edges(tfield)
        edges(hfield)
        place(tfield, 1, flat, tf)
        for c in th:
            c.wait()
        place(tfield, 0, ordered(thalo[0]) * first, 1)
        place(tfield, tf + 1, ordered(thalo[1]) * final, 1)
        for k in range(27):
            a, b, c = k // 9, k // 3 % 3, k % 3
            im1[:, k * width:(k + 1) * width] = (
                tfield[b, a:a + tf, c:c + cols].reshape(n, width))
        cp1.wait()
        z = jnp.dot(im1[...], w1[...], preferred_element_type=F32) + b1[...]
        th_ = jnp.tanh(GELU_ROOT * (z + GELU_CUBE * z * z * z))
        slope = 0.5 * (1.0 + th_) + 0.5 * z * (1.0 - th_ * th_) * GELU_ROOT * (
            1.0 + 3.0 * GELU_CUBE * z * z)
        hid = (0.5 * z * (1.0 + th_)).astype(BF16)
        hsend[...] = hid.reshape(tf, cols, rows, mid)
        hh = halo(hsend.at[0], hsend.at[tf - 1], hhalo, hh_s, hh_r)
        for c in hh:
            c.start()
        hid_f = hid.astype(F32)
        place(hfield, 1, hid_f, tf)

        own.wait()
        finish(nseq, px_copy, px_arrival)
        pix_rows = pxall[...].astype(F32).reshape(n, 4 * values).astype(BF16)
        px = jnp.dot(perm[...], pix_rows, preferred_element_type=F32)
        center = px - jnp.mean(px, axis=-1, keepdims=True)
        spread = jnp.mean(center * center, axis=-1, keepdims=True)
        normed = center * lax.rsqrt(spread + 1e-06)

        for c in hh:
            c.wait()
        before = hhalo[0].reshape(plane, mid).astype(F32) * first
        after = hhalo[1].reshape(plane, mid).astype(F32) * final
        place(hfield, 0, before, 1)
        place(hfield, tf + 1, after, 1)

        for ij in range(4):
            i, j = ij // 2, ij % 2
            for k in range(27):
                a, b, c = k // 9, k // 3 % 3, k % 3
                dh, dw = floor_half(i + b - 1), floor_half(j + c - 1)
                im2[ij * n:(ij + 1) * n, k * mid:(k + 1) * mid] = (
                    hfield[dh + 1, a:a + tf, dw + 1:dw + 1 + cols].reshape(n, mid))
        cp2.wait()
        predict = jnp.dot(im2[...], w2[...], preferred_element_type=F32) + b2[...].reshape(1, values)
        cots = []
        for ij in range(4):
            cot = (scale * (predict[ij * n:(ij + 1) * n]
                            - normed[:, ij * values:(ij + 1) * values])).astype(BF16).astype(F32)
            cots.append(cot)
            turned = cot.T
            for d in range(ndp):
                csend[d, ij] = turned[d * vblk:(d + 1) * vblk].astype(BF16)
        time_line = jnp.concatenate([before, hid_f, after], axis=0)
        for a in range(3):
            htsend[a * mid:(a + 1) * mid] = (
                time_line[a * plane:a * plane + n].T.astype(BF16))
        each(ndp, lambda o: [c.start() for c in c_pair(o)])
        call_[dp] = csend[dp]
        htall[dp] = htsend[...]

        def pair_sums(low, high, shift):
            return (high + shift(low, 1), low + high, shift(high, -1) + low)

        def cell_sums(parts, rshift, cshift):
            by_col = [pair_sums(parts[j], parts[2 + j], rshift) for j in range(2)]
            return [s for b in range(3)
                    for s in pair_sums(by_col[0][b], by_col[1][b], cshift)]

        sums = [s.astype(BF16) for s in cell_sums(cots, row_shift, col_shift)]
        backs = []
        for a in range(3):
            total = jnp.zeros((n, mid), F32)
            for bc in range(9):
                k = a * 9 + bc
                total = total + lax.dot_general(
                    sums[bc], w2[k * mid:(k + 1) * mid], NT, preferred_element_type=F32)
            backs.append(total)
        psend[0] = backs[2][n - plane:]
        psend[1] = backs[0][:plane]
        ph = halo(psend.at[1], psend.at[0], phalo, ph_s, ph_r)
        for c in ph:
            c.start()
        for c in ph:
            c.wait()
        from_prev, from_next = phalo[0] * first, phalo[1] * final
        if tf > 1:
            late = jnp.concatenate([from_prev, backs[2][:n - plane]], axis=0)
            early = jnp.concatenate([backs[0][plane:], from_next], axis=0)
        else:
            late, early = from_prev, from_next
        grad_z = ((backs[1] + late + early) * slope).astype(BF16).astype(F32).T
        for d in range(ndp):
            gsend[d] = grad_z[d * cblk:(d + 1) * cblk].astype(BF16)
        start_all(ndev, g_copy)
        gall[me] = gsend[dp]

        each(ndp, lambda o: [c.wait_send() for c in c_pair(o)])
        each(ndp, lambda o: [c.wait_recv() for c in c_arrival(o)])

        def lane_row(v, d):
            rolled = pltpu.roll(v, 1 if d < 0 else n - 1, axis=1)
            return rolled * (lanes_n[0:1] if d < 0 else lanes_n[1:2])

        def lane_col(v, d):
            rolled = pltpu.roll(v, rows if d < 0 else n - rows, axis=1)
            return rolled * (lanes_n[2:3] if d < 0 else lanes_n[3:4])

        acc[...] = jnp.zeros_like(acc)

        def one_clip(q, carry):
            parts = [call_[q, ij].astype(F32) for ij in range(4)]
            stack = jnp.concatenate(cell_sums(parts, lane_row, lane_col), axis=0).astype(BF16)
            acc[...] += lax.dot_general(htall[q], stack, NT, preferred_element_type=F32)
            return carry

        lax.fori_loop(0, ndp, one_clip, 0)
        for s in range(nseq):
            for a in range(3):
                lo = a * mid + s * mblk
                rsend[s, a] = acc[lo:lo + mblk].astype(BF16)
        start_all(nseq, r_copy)
        rall[seq] = rsend[seq]

        finish(ndev, x_copy, x_arrival)
        finish(ndev, g_copy, g_arrival)
        o1[...] = jnp.zeros_like(o1)

        def one_first(q, carry):
            base = q * nseq
            g = jnp.concatenate([gall[base + s].astype(F32) for s in range(nseq)], axis=1)
            x = jnp.concatenate([xall[base + s] for s in range(nseq)], axis=1)
            pieces = []
            by_row = []
            for b in range(3):
                d = b - 1
                if d == 0:
                    by_row.append(g)
                else:
                    m = pltpu.roll(g, d % clip_lanes, axis=1)
                    by_row.append(m * (lanev[0:1] if d > 0 else lanev[1:2]))
            grid = {}
            for b in range(3):
                for c in range(3):
                    d = c - 1
                    v = by_row[b]
                    if d != 0:
                        v = pltpu.roll(v, (d * rows) % clip_lanes, axis=1)
                        v = v * (lanev[2:3] if d > 0 else lanev[3:4])
                    grid[b, c] = v
            for a in range(3):
                for b in range(3):
                    for c in range(3):
                        d = a - 1
                        v = grid[b, c]
                        if d != 0:
                            v = pltpu.roll(v, (d * plane) % clip_lanes, axis=1)
                            v = v * (lanev[4:5] if d > 0 else lanev[5:6])
                        pieces.append(v)
            stack = jnp.concatenate(pieces, axis=0).astype(BF16)
            o1[...] += lax.dot_general(stack, x, NT, preferred_element_type=F32)
            return carry

        lax.fori_loop(0, ndp, one_first, 0)

        finish(nseq, r_copy, r_arrival)
        total = rall[0].astype(F32)
        for s in range(1, nseq):
            total = total + rall[s].astype(F32)
        for a in range(3):
            for bc in range(9):
                o2[a * 9 + bc] = total[a, :, bc * vblk:(bc + 1) * vblk]

    return kernel


def per_device(tokens, conv_first, bias_first, conv_second, bias_second, pixels, mask_index):
    ndp, nseq = lax.axis_size("dp"), lax.axis_size("seq")
    tf, rows, cols, width = tokens.shape[1:]
    frames = tf * nseq
    mid, values = conv_second.shape[1], conv_second.shape[2]
    n = tf * rows * cols
    hb = rows // nseq
    dims = (ndp, nseq, frames, tf, rows, cols, width, mid, values)
    plane = rows * cols
    dblk, cblk, vblk, mblk = width // nseq, mid // ndp, values // ndp, mid // nseq
    ndev = ndp * nseq

    idx = np.arange(n, dtype=np.int32)
    t_of, w_of, h_of = idx // plane, idx // rows % cols, idx % rows
    source = (h_of // hb) * (tf * hb * cols) + t_of * (hb * cols) + (h_of % hb) * cols + w_of
    perm = jnp.asarray(source[:, None] == idx[None, :], BF16)
    flat_place = (h_of * cols + w_of)[:plane]
    tperm = jnp.asarray(flat_place[:, None] == idx[None, :plane], BF16)
    place_of = jnp.asarray((h_of * cols + w_of)[:, None])
    colv = jnp.asarray(np.stack([h_of < 0, h_of > 0, h_of < rows - 1,
                                 w_of > 0, w_of < cols - 1], axis=1), F32)
    lanes_n = jnp.asarray(np.stack([h_of > 0, h_of < rows - 1, w_of > 0, w_of < cols - 1]), F32)
    lid = np.arange(frames * plane, dtype=np.int32)
    tl, wl, hl = lid // plane, lid // rows % cols, lid % rows
    lanev = jnp.asarray(np.stack([hl > 0, hl < rows - 1, wl > 0, wl < cols - 1,
                                  tl > 0, tl < frames - 1]), F32)

    vm = pl.BlockSpec(memory_space=pltpu.VMEM)
    hbm = pl.BlockSpec(memory_space=pl.ANY)

    def dma(k):
        return pltpu.SemaphoreType.DMA((k,))

    scratch = [
        pltpu.VMEM((27 * width, mid), BF16),
        pltpu.VMEM((27 * mid, values), BF16),
        pltpu.VMEM((nseq, dblk, n), BF16),
        pltpu.VMEM((ndev, dblk, n), BF16),
        pltpu.VMEM((2, rows, cols, width), BF16),
        pltpu.VMEM((nseq, tf, hb, cols, 4 * values), BF16),
        pltpu.VMEM((3, tf + 2, cols + 2, rows, width), BF16),
        pltpu.VMEM((n, 27 * width), BF16),
        pltpu.VMEM((tf, cols, rows, mid), BF16),
        pltpu.VMEM((2, cols, rows, mid), BF16),
        pltpu.VMEM((3, tf + 2, cols + 2, rows, mid), BF16),
        pltpu.VMEM((4 * n, 27 * mid), BF16),
        pltpu.VMEM((2, plane, mid), F32),
        pltpu.VMEM((2, plane, mid), F32),
        pltpu.VMEM((ndp, 4, vblk, n), BF16),
        pltpu.VMEM((ndp, 4, vblk, n), BF16),
        pltpu.VMEM((3 * mid, n), BF16),
        pltpu.VMEM((ndp, 3 * mid, n), BF16),
        pltpu.VMEM((nseq, 3, mblk, 9 * vblk), BF16),
        pltpu.VMEM((nseq, 3, mblk, 9 * vblk), BF16),
        pltpu.VMEM((ndp, cblk, n), BF16),
        pltpu.VMEM((ndev, cblk, n), BF16),
        pltpu.VMEM((3 * mid, 9 * vblk), F32),
        dma(3), dma(2), dma(2), dma(nseq), dma(nseq), dma(ndev), dma(ndev),
        dma(2), dma(2), dma(2), dma(2), dma(ndp), dma(ndp), dma(ndp), dma(ndp),
        dma(nseq), dma(nseq), dma(ndev), dma(ndev),
    ]
    first, second = pl.pallas_call(
        make_kernel(dims),
        out_shape=(jax.ShapeDtypeStruct((27 * cblk, dblk), F32),
                   jax.ShapeDtypeStruct((27, mblk, vblk), F32)),
        in_specs=[vm, hbm, vm, hbm, vm, hbm, vm, vm, vm, vm, vm, vm, vm],
        out_specs=(vm, vm),
        scratch_shapes=scratch,
        compiler_params=pltpu.CompilerParams(
            collective_id=0, has_side_effects=True, vmem_limit_bytes=60 * 1024 * 1024),
        name="step",
    )(tokens[0], conv_first.reshape(27 * width, mid), bias_first.reshape(1, mid),
      conv_second.reshape(27 * mid, values), bias_second,
      pixels[0], mask_index, place_of, tperm, perm, colv, lanev, lanes_n)
    first = first.reshape(27, cblk, dblk).transpose(0, 2, 1)
    return (first, second)


def solution(mesh):
    return jax.shard_map(
        per_device,
        mesh=mesh,
        in_specs=(
            P("dp", "seq", None, None, None),
            P(),
            P(),
            P(),
            P(),
            P("dp", None, "seq", None, None),
            P("dp", None),
        ),
        out_specs=(P(None, "seq", "dp"), P(None, "seq", "dp")),
        check_vma=False,
    )
```

```python
import jax
import jax.numpy as jnp
import numpy as np
from jax import lax
from jax.experimental import pallas as pl
from jax.experimental.pallas import tpu as pltpu
from jax.sharding import PartitionSpec as P

F32 = jnp.float32
BF16 = jnp.bfloat16
NT = (((1,), (1,)), ((), ()))
GELU_ROOT = 0.7978845608028654
GELU_CUBE = 0.044715


def floor_half(v):
    return v // 2 if v >= 0 else -1


def make_kernel(dims):
    ndp, nseq, frames, tf, rows, cols, width, mid, values = dims
    n = tf * cols * rows
    plane = cols * rows
    dblk = width // nseq
    cblk = mid // ndp
    vblk = values // ndp
    mblk = mid // nseq
    ndev = ndp * nseq
    nz = nseq // 2
    half = ndev // 2
    clip_lanes = nseq * n

    def kernel(tok, w1_hbm, b1, w2_hbm, b2, pix, marks, place_of, tperm, perm, colv, lanev,
               lanes_n, o1, o2,
               w1, w2, xbuf, xall, thalo, pxall, tfield, im1, hsend, hhalo, hfield, im2,
               psend, phalo, csend, call_, htsend, htall, qsend, qrecv, rsend, rall, gsend, gall, acc,
               wsem, th_s, th_r, px_s, px_r, x_s, x_r, hh_s, hh_r, ph_s, ph_r,
               c_s, c_r, ht_s, ht_r, q_s, q_r, r_s, r_r, g_s, g_r):
        dp = lax.axis_index("dp")
        seq = lax.axis_index("seq")
        me = dp * nseq + seq
        chip, core = seq // 2, lax.rem(seq, 2)
        nxt = lax.rem(seq + 1, nseq)
        prv = lax.rem(seq + nseq - 1, nseq)

        def remote(src, dst, ss, rs, d, s):
            return pltpu.make_async_remote_copy(
                src_ref=src, dst_ref=dst, send_sem=ss, recv_sem=rs,
                device_id=(d, s), device_id_type=pl.DeviceIdType.MESH)

        cp1 = pltpu.make_async_copy(w1_hbm, w1, wsem.at[0])
        cp2 = pltpu.make_async_copy(w2_hbm, w2, wsem.at[1])
        cp1.start()
        cp2.start()

        barrier = pltpu.get_barrier_semaphore()

        def greet(o, c):
            t = lax.rem(me + o, ndev)
            pl.semaphore_signal(barrier, inc=1, device_id=(t // nseq, lax.rem(t, nseq)),
                                device_id_type=pl.DeviceIdType.MESH)
            return c

        lax.fori_loop(1, ndev, greet, 0)

        def ordered(frame):
            raw = frame.astype(F32).reshape(plane, width).astype(BF16)
            return jnp.dot(tperm[...], raw, preferred_element_type=F32)

        flat = jnp.concatenate([ordered(tok[t]) for t in range(tf)], axis=0)
        xt = flat.T
        for s in range(nseq):
            xbuf[s] = xt[s * dblk:(s + 1) * dblk].astype(BF16)
        pl.semaphore_wait(barrier, ndev - 1)

        def halo(first, last, dst, ss, rs):
            return (remote(last, dst.at[0], ss.at[0], rs.at[0], dp, nxt),
                    remote(first, dst.at[1], ss.at[1], rs.at[1], dp, prv))

        th = halo(tok.at[0], tok.at[tf - 1], thalo, th_s, th_r)
        for c in th:
            c.start()

        def px_copy(o):
            s = lax.rem(seq + o, nseq)
            return remote(pix.at[pl.ds(s * tf, tf)], pxall.at[seq], px_s.at[o], px_r.at[seq],
                          dp, s)

        def px_arrival(o):
            s = lax.rem(seq + nseq - o, nseq)
            return remote(pix.at[pl.ds(s * tf, tf)], pxall.at[s], px_s.at[o], px_r.at[s], dp, s)

        def x_copy(o):
            t = lax.rem(me + o, ndev)
            s = lax.rem(t, nseq)
            return remote(xbuf.at[s], xall.at[me], x_s.at[o], x_r.at[me], t // nseq, s)

        def x_arrival(o):
            t = lax.rem(me + ndev - o, ndev)
            s = lax.rem(t, nseq)
            return remote(xbuf.at[s], xall.at[t], x_s.at[o], x_r.at[t], t // nseq, s)

        def c_pair(o):
            d = lax.rem(dp + o, ndp)
            return (remote(csend.at[d], call_.at[dp], c_s.at[o], c_r.at[dp], d, seq),
                    remote(htsend, htall.at[dp], ht_s.at[o], ht_r.at[dp], d, seq))

        def c_arrival(o):
            d = lax.rem(dp + ndp - o, ndp)
            return (remote(csend.at[d], call_.at[d], c_s.at[o], c_r.at[d], d, seq),
                    remote(htsend, htall.at[d], ht_s.at[o], ht_r.at[d], d, seq))

        def r_copy(o):
            s = lax.rem(chip + o, nz)
            return remote(rsend.at[s], rall.at[chip], r_s.at[o], r_r.at[chip], dp,
                          s * 2 + core)

        def r_arrival(o):
            s = lax.rem(chip + nz - o, nz)
            return remote(rsend.at[s], rall.at[s], r_s.at[o], r_r.at[s], dp, s * 2 + core)

        def g_copy(o):
            t = lax.rem(me + o, ndev)
            d = t // nseq
            return remote(gsend.at[d], gall.at[me], g_s.at[o], g_r.at[me], d, lax.rem(t, nseq))

        def g_arrival(o):
            t = lax.rem(me + ndev - o, ndev)
            d = t // nseq
            return remote(gsend.at[d], gall.at[t], g_s.at[o], g_r.at[t], d, lax.rem(t, nseq))

        def each(count, act, low=1):
            def body(o, c):
                act(o)
                return c
            lax.fori_loop(low, count, body, 0)

        def start_all(count, copy, low=1):
            each(count, lambda o: copy(o).start(), low)

        def finish(count, copy, arrival):
            each(count, lambda o: copy(o).wait_send())
            each(count, lambda o: arrival(o).wait_recv())

        start_all(nseq, px_copy)
        xall[me] = xbuf[seq]
        own = pltpu.make_async_copy(pix.at[pl.ds(seq * tf, tf)], pxall.at[seq], wsem.at[2])
        own.start()

        matches = (place_of[...] == marks[...]).astype(F32)
        scale = 2.0 / (4 * values) * jnp.sum(matches, axis=1, keepdims=True)
        h_low, h_high = colv[:, 1:2], colv[:, 2:3]
        w_low, w_high = colv[:, 3:4], colv[:, 4:5]

        def row_shift(v, d):
            m = v.shape[0]
            if d == 0:
                return v
            rolled = pltpu.roll(v, 1 if d < 0 else m - 1, axis=0)
            return rolled * (h_low if d < 0 else h_high)[:m]

        def col_shift(v, d):
            m = v.shape[0]
            if d == 0:
                return v
            rolled = pltpu.roll(v, rows if d < 0 else m - rows, axis=0)
            return rolled * (w_low if d < 0 else w_high)[:m]

        def place(field, frame, v, count):
            for d in (-1, 0, 1):
                field[d + 1, frame:frame + count, 1:cols + 1] = (
                    row_shift(v, d).astype(BF16).reshape(count, cols, rows, v.shape[1]))

        def edges(field):
            zero = jnp.zeros((3, tf + 2, 1, rows, field.shape[4]), BF16)
            field[:, :, 0:1] = zero
            field[:, :, cols + 1:cols + 2] = zero

        first = jnp.where(seq > 0, 1.0, 0.0).astype(F32)
        final = jnp.where(seq < nseq - 1, 1.0, 0.0).astype(F32)

        edges(tfield)
        edges(hfield)
        place(tfield, 1, flat, tf)
        for c in th:
            c.wait()
        place(tfield, 0, ordered(thalo[0]) * first, 1)
        place(tfield, tf + 1, ordered(thalo[1]) * final, 1)
        for k in range(27):
            a, b, c = k // 9, k // 3 % 3, k % 3
            im1[:, k * width:(k + 1) * width] = (
                tfield[b, a:a + tf, c:c + cols].reshape(n, width))
        cp1.wait()
        z = jnp.dot(im1[...], w1[...], preferred_element_type=F32) + b1[...]
        th_ = jnp.tanh(GELU_ROOT * (z + GELU_CUBE * z * z * z))
        slope = 0.5 * (1.0 + th_) + 0.5 * z * (1.0 - th_ * th_) * GELU_ROOT * (
            1.0 + 3.0 * GELU_CUBE * z * z)
        hid = (0.5 * z * (1.0 + th_)).astype(BF16)
        hsend[...] = hid.reshape(tf, cols, rows, mid)
        hh = halo(hsend.at[0], hsend.at[tf - 1], hhalo, hh_s, hh_r)
        for c in hh:
            c.start()
        hid_f = hid.astype(F32)
        place(hfield, 1, hid_f, tf)

        own.wait()
        finish(nseq, px_copy, px_arrival)
        pix_rows = pxall[...].astype(F32).reshape(n, 4 * values).astype(BF16)
        px = jnp.dot(perm[...], pix_rows, preferred_element_type=F32)
        center = px - jnp.mean(px, axis=-1, keepdims=True)
        spread = jnp.mean(center * center, axis=-1, keepdims=True)
        normed = center * lax.rsqrt(spread + 1e-06)

        for c in hh:
            c.wait()
        start_all(half, x_copy)
        before = hhalo[0].reshape(plane, mid).astype(F32) * first
        after = hhalo[1].reshape(plane, mid).astype(F32) * final
        place(hfield, 0, before, 1)
        place(hfield, tf + 1, after, 1)

        for ij in range(4):
            i, j = ij // 2, ij % 2
            for k in range(27):
                a, b, c = k // 9, k // 3 % 3, k % 3
                dh, dw = floor_half(i + b - 1), floor_half(j + c - 1)
                im2[ij * n:(ij + 1) * n, k * mid:(k + 1) * mid] = (
                    hfield[dh + 1, a:a + tf, dw + 1:dw + 1 + cols].reshape(n, mid))
        cp2.wait()
        predict = jnp.dot(im2[...], w2[...], preferred_element_type=F32) + b2[...].reshape(1, values)
        cots = []
        for ij in range(4):
            cot = (scale * (predict[ij * n:(ij + 1) * n]
                            - normed[:, ij * values:(ij + 1) * values])).astype(BF16).astype(F32)
            cots.append(cot)
            turned = cot.T
            for d in range(ndp):
                csend[d, ij] = turned[d * vblk:(d + 1) * vblk].astype(BF16)
        time_line = jnp.concatenate([before, hid_f, after], axis=0)
        for a in range(3):
            htsend[a * mid:(a + 1) * mid] = (
                time_line[a * plane:a * plane + n].T.astype(BF16))
        each(ndp, lambda o: [c.start() for c in c_pair(o)])
        call_[dp] = csend[dp]
        htall[dp] = htsend[...]

        def pair_sums(low, high, shift):
            return (high + shift(low, 1), low + high, shift(high, -1) + low)

        def cell_sums(parts, rshift, cshift):
            by_col = [pair_sums(parts[j], parts[2 + j], rshift) for j in range(2)]
            return [s for b in range(3)
                    for s in pair_sums(by_col[0][b], by_col[1][b], cshift)]

        sums = [s.astype(BF16) for s in cell_sums(cots, row_shift, col_shift)]
        backs = []
        for a in range(3):
            total = jnp.zeros((n, mid), F32)
            for bc in range(9):
                k = a * 9 + bc
                total = total + lax.dot_general(
                    sums[bc], w2[k * mid:(k + 1) * mid], NT, preferred_element_type=F32)
            backs.append(total)
        psend[0] = backs[2][n - plane:]
        psend[1] = backs[0][:plane]
        ph = halo(psend.at[1], psend.at[0], phalo, ph_s, ph_r)
        for c in ph:
            c.start()
        for c in ph:
            c.wait()
        from_prev, from_next = phalo[0] * first, phalo[1] * final
        if tf > 1:
            late = jnp.concatenate([from_prev, backs[2][:n - plane]], axis=0)
            early = jnp.concatenate([backs[0][plane:], from_next], axis=0)
        else:
            late, early = from_prev, from_next
        grad_z = ((backs[1] + late + early) * slope).astype(BF16).astype(F32).T
        for d in range(ndp):
            gsend[d] = grad_z[d * cblk:(d + 1) * cblk].astype(BF16)
        start_all(ndev, g_copy)
        start_all(ndev, x_copy, half)
        gall[me] = gsend[dp]

        each(ndp, lambda o: [c.wait_send() for c in c_pair(o)])
        each(ndp, lambda o: [c.wait_recv() for c in c_arrival(o)])

        def lane_row(v, d):
            rolled = pltpu.roll(v, 1 if d < 0 else n - 1, axis=1)
            return rolled * (lanes_n[0:1] if d < 0 else lanes_n[1:2])

        def lane_col(v, d):
            rolled = pltpu.roll(v, rows if d < 0 else n - rows, axis=1)
            return rolled * (lanes_n[2:3] if d < 0 else lanes_n[3:4])

        acc[...] = jnp.zeros_like(acc)

        def one_clip(q, carry):
            parts = [call_[q, ij].astype(F32) for ij in range(4)]
            stack = jnp.concatenate(cell_sums(parts, lane_row, lane_col), axis=0).astype(BF16)
            acc[...] += lax.dot_general(htall[q], stack, NT, preferred_element_type=F32)
            return carry

        lax.fori_loop(0, ndp, one_clip, 0)

        def part(a, s):
            return acc[pl.ds(pl.multiple_of(a * mid + s * mblk, 8), mblk)]

        for s in range(nz):
            for a in range(3):
                qsend[s, a] = part(a, 2 * s + 1 - core).astype(BF16)
        swap = remote(qsend, qrecv, q_s.at[0], q_r.at[0], dp, 2 * chip + 1 - core)
        swap.start()
        swap.wait()
        for s in range(nz):
            for a in range(3):
                rsend[s, a] = (part(a, 2 * s + core) + qrecv[s, a].astype(F32)).astype(BF16)
        start_all(nz, r_copy)
        rall[chip] = rsend[chip]

        finish(ndev, x_copy, x_arrival)
        finish(ndev, g_copy, g_arrival)
        o1[...] = jnp.zeros_like(o1)

        def one_first(q, carry):
            base = q * nseq
            g = jnp.concatenate([gall[base + s].astype(F32) for s in range(nseq)], axis=1)
            x = jnp.concatenate([xall[base + s] for s in range(nseq)], axis=1)
            pieces = []
            by_row = []
            for b in range(3):
                d = b - 1
                if d == 0:
                    by_row.append(g)
                else:
                    m = pltpu.roll(g, d % clip_lanes, axis=1)
                    by_row.append(m * (lanev[0:1] if d > 0 else lanev[1:2]))
            grid = {}
            for b in range(3):
                for c in range(3):
                    d = c - 1
                    v = by_row[b]
                    if d != 0:
                        v = pltpu.roll(v, (d * rows) % clip_lanes, axis=1)
                        v = v * (lanev[2:3] if d > 0 else lanev[3:4])
                    grid[b, c] = v
            for a in range(3):
                for b in range(3):
                    for c in range(3):
                        d = a - 1
                        v = grid[b, c]
                        if d != 0:
                            v = pltpu.roll(v, (d * plane) % clip_lanes, axis=1)
                            v = v * (lanev[4:5] if d > 0 else lanev[5:6])
                        pieces.append(v)
            stack = jnp.concatenate(pieces, axis=0).astype(BF16)
            o1[...] += lax.dot_general(stack, x, NT, preferred_element_type=F32)
            return carry

        lax.fori_loop(0, ndp, one_first, 0)

        finish(nz, r_copy, r_arrival)
        total = rall[0].astype(F32)
        for s in range(1, nz):
            total = total + rall[s].astype(F32)
        for a in range(3):
            for bc in range(9):
                o2[a * 9 + bc] = total[a, :, bc * vblk:(bc + 1) * vblk]

    return kernel


def per_device(tokens, conv_first, bias_first, conv_second, bias_second, pixels, mask_index):
    ndp, nseq = lax.axis_size("dp"), lax.axis_size("seq")
    tf, rows, cols, width = tokens.shape[1:]
    frames = tf * nseq
    mid, values = conv_second.shape[1], conv_second.shape[2]
    n = tf * rows * cols
    hb = rows // nseq
    dims = (ndp, nseq, frames, tf, rows, cols, width, mid, values)
    plane = rows * cols
    dblk, cblk, vblk, mblk = width // nseq, mid // ndp, values // ndp, mid // nseq
    ndev = ndp * nseq

    idx = np.arange(n, dtype=np.int32)
    t_of, w_of, h_of = idx // plane, idx // rows % cols, idx % rows
    source = (h_of // hb) * (tf * hb * cols) + t_of * (hb * cols) + (h_of % hb) * cols + w_of
    perm = jnp.asarray(source[:, None] == idx[None, :], BF16)
    flat_place = (h_of * cols + w_of)[:plane]
    tperm = jnp.asarray(flat_place[:, None] == idx[None, :plane], BF16)
    place_of = jnp.asarray((h_of * cols + w_of)[:, None])
    colv = jnp.asarray(np.stack([h_of < 0, h_of > 0, h_of < rows - 1,
                                 w_of > 0, w_of < cols - 1], axis=1), F32)
    lanes_n = jnp.asarray(np.stack([h_of > 0, h_of < rows - 1, w_of > 0, w_of < cols - 1]), F32)
    lid = np.arange(frames * plane, dtype=np.int32)
    tl, wl, hl = lid // plane, lid // rows % cols, lid % rows
    lanev = jnp.asarray(np.stack([hl > 0, hl < rows - 1, wl > 0, wl < cols - 1,
                                  tl > 0, tl < frames - 1]), F32)

    vm = pl.BlockSpec(memory_space=pltpu.VMEM)
    hbm = pl.BlockSpec(memory_space=pl.ANY)

    def dma(k):
        return pltpu.SemaphoreType.DMA((k,))

    scratch = [
        pltpu.VMEM((27 * width, mid), BF16),
        pltpu.VMEM((27 * mid, values), BF16),
        pltpu.VMEM((nseq, dblk, n), BF16),
        pltpu.VMEM((ndev, dblk, n), BF16),
        pltpu.VMEM((2, rows, cols, width), BF16),
        pltpu.VMEM((nseq, tf, hb, cols, 4 * values), BF16),
        pltpu.VMEM((3, tf + 2, cols + 2, rows, width), BF16),
        pltpu.VMEM((n, 27 * width), BF16),
        pltpu.VMEM((tf, cols, rows, mid), BF16),
        pltpu.VMEM((2, cols, rows, mid), BF16),
        pltpu.VMEM((3, tf + 2, cols + 2, rows, mid), BF16),
        pltpu.VMEM((4 * n, 27 * mid), BF16),
        pltpu.VMEM((2, plane, mid), F32),
        pltpu.VMEM((2, plane, mid), F32),
        pltpu.VMEM((ndp, 4, vblk, n), BF16),
        pltpu.VMEM((ndp, 4, vblk, n), BF16),
        pltpu.VMEM((3 * mid, n), BF16),
        pltpu.VMEM((ndp, 3 * mid, n), BF16),
        pltpu.VMEM((nseq // 2, 3, mblk, 9 * vblk), BF16),
        pltpu.VMEM((nseq // 2, 3, mblk, 9 * vblk), BF16),
        pltpu.VMEM((nseq // 2, 3, mblk, 9 * vblk), BF16),
        pltpu.VMEM((nseq // 2, 3, mblk, 9 * vblk), BF16),
        pltpu.VMEM((ndp, cblk, n), BF16),
        pltpu.VMEM((ndev, cblk, n), BF16),
        pltpu.VMEM((3 * mid, 9 * vblk), F32),
        dma(3), dma(2), dma(2), dma(nseq), dma(nseq), dma(ndev), dma(ndev),
        dma(2), dma(2), dma(2), dma(2), dma(ndp), dma(ndp), dma(ndp), dma(ndp),
        dma(1), dma(1), dma(nseq // 2), dma(nseq // 2), dma(ndev), dma(ndev),
    ]
    first, second = pl.pallas_call(
        make_kernel(dims),
        out_shape=(jax.ShapeDtypeStruct((27 * cblk, dblk), F32),
                   jax.ShapeDtypeStruct((27, mblk, vblk), F32)),
        in_specs=[vm, hbm, vm, hbm, vm, hbm, vm, vm, vm, vm, vm, vm, vm],
        out_specs=(vm, vm),
        scratch_shapes=scratch,
        compiler_params=pltpu.CompilerParams(
            collective_id=0, has_side_effects=True, vmem_limit_bytes=60 * 1024 * 1024),
        name="step",
    )(tokens[0], conv_first.reshape(27 * width, mid), bias_first.reshape(1, mid),
      conv_second.reshape(27 * mid, values), bias_second,
      pixels[0], mask_index, place_of, tperm, perm, colv, lanev, lanes_n)
    first = first.reshape(27, cblk, dblk).transpose(0, 2, 1)
    return (first, second)


def solution(mesh):
    return jax.shard_map(
        per_device,
        mesh=mesh,
        in_specs=(
            P("dp", "seq", None, None, None),
            P(),
            P(),
            P(),
            P(),
            P("dp", None, "seq", None, None),
            P("dp", None),
        ),
        out_specs=(P(None, "seq", "dp"), P(None, "seq", "dp")),
        check_vma=False,
    )
```

```python
import jax
import jax.numpy as jnp
import numpy as np
from jax import lax
from jax.experimental import pallas as pl
from jax.experimental.pallas import tpu as pltpu
from jax.sharding import PartitionSpec as P

F32 = jnp.float32
BF16 = jnp.bfloat16
NT = (((1,), (1,)), ((), ()))
GELU_ROOT = 0.7978845608028654
GELU_CUBE = 0.044715


def floor_half(v):
    return v // 2 if v >= 0 else -1


def make_kernel(dims):
    ndp, nseq, frames, tf, rows, cols, width, mid, values = dims
    n = tf * cols * rows
    plane = cols * rows
    dblk = width // nseq
    cblk = mid // ndp
    vblk = values // ndp
    mblk = mid // nseq
    ndev = ndp * nseq
    nz = nseq // 2
    half = ndev // 2
    clip_lanes = nseq * n

    def kernel(tok, w1_hbm, b1, w2_hbm, b2, pix, marks, place_of, tperm, perm, colv, lanev,
               lanes_n, o1, o2,
               w1, w2, xbuf, xall, thalo, pxall, tfield, im1, hsend, hhalo, hfield, im2,
               psend, phalo, csend, call_, htsend, htall, qsend, qrecv, rsend, rall, gsend, gall, acc,
               wsem, th_s, th_r, px_s, px_r, x_s, x_r, hh_s, hh_r, ph_s, ph_r,
               c_s, c_r, ht_s, ht_r, q_s, q_r, r_s, r_r, g_s, g_r):
        dp = lax.axis_index("dp")
        seq = lax.axis_index("seq")
        me = dp * nseq + seq
        chip, core = seq // 2, lax.rem(seq, 2)
        nxt = lax.rem(seq + 1, nseq)
        prv = lax.rem(seq + nseq - 1, nseq)

        def remote(src, dst, ss, rs, d, s):
            return pltpu.make_async_remote_copy(
                src_ref=src, dst_ref=dst, send_sem=ss, recv_sem=rs,
                device_id=(d, s), device_id_type=pl.DeviceIdType.MESH)

        cp1 = pltpu.make_async_copy(w1_hbm, w1, wsem.at[0])
        cp2 = pltpu.make_async_copy(w2_hbm, w2, wsem.at[1])
        cp1.start()
        cp2.start()

        barrier = pltpu.get_barrier_semaphore()

        def greet(o, c):
            t = lax.rem(me + o, ndev)
            pl.semaphore_signal(barrier, inc=1, device_id=(t // nseq, lax.rem(t, nseq)),
                                device_id_type=pl.DeviceIdType.MESH)
            return c

        lax.fori_loop(1, ndev, greet, 0)

        def ordered(frame):
            raw = frame.astype(F32).reshape(plane, width).astype(BF16)
            return jnp.dot(tperm[...], raw, preferred_element_type=F32)

        flat = jnp.concatenate([ordered(tok[t]) for t in range(tf)], axis=0)
        xt = flat.T
        for s in range(nseq):
            xbuf[s] = xt[s * dblk:(s + 1) * dblk].astype(BF16)
        pl.semaphore_wait(barrier, ndev - 1)

        def halo(first, last, dst, ss, rs):
            return (remote(last, dst.at[0], ss.at[0], rs.at[0], dp, nxt),
                    remote(first, dst.at[1], ss.at[1], rs.at[1], dp, prv))

        th = halo(tok.at[0], tok.at[tf - 1], thalo, th_s, th_r)
        for c in th:
            c.start()

        def px_copy(o):
            s = lax.rem(seq + o, nseq)
            return remote(pix.at[pl.ds(s * tf, tf)], pxall.at[seq], px_s.at[o], px_r.at[seq],
                          dp, s)

        def px_arrival(o):
            s = lax.rem(seq + nseq - o, nseq)
            return remote(pix.at[pl.ds(s * tf, tf)], pxall.at[s], px_s.at[o], px_r.at[s], dp, s)

        def x_copy(o):
            t = lax.rem(me + o, ndev)
            s = lax.rem(t, nseq)
            return remote(xbuf.at[s], xall.at[me], x_s.at[o], x_r.at[me], t // nseq, s)

        def x_arrival(o):
            t = lax.rem(me + ndev - o, ndev)
            s = lax.rem(t, nseq)
            return remote(xbuf.at[s], xall.at[t], x_s.at[o], x_r.at[t], t // nseq, s)

        def c_pair(o):
            d = lax.rem(dp + o, ndp)
            return (remote(csend.at[d], call_.at[dp], c_s.at[o], c_r.at[dp], d, seq),
                    remote(htsend, htall.at[dp], ht_s.at[o], ht_r.at[dp], d, seq))

        def c_arrival(o):
            d = lax.rem(dp + ndp - o, ndp)
            return (remote(csend.at[d], call_.at[d], c_s.at[o], c_r.at[d], d, seq),
                    remote(htsend, htall.at[d], ht_s.at[o], ht_r.at[d], d, seq))

        def r_copy(o):
            s = lax.rem(chip + o, nz)
            return remote(rsend.at[s], rall.at[chip], r_s.at[o], r_r.at[chip], dp,
                          s * 2 + core)

        def r_arrival(o):
            s = lax.rem(chip + nz - o, nz)
            return remote(rsend.at[s], rall.at[s], r_s.at[o], r_r.at[s], dp, s * 2 + core)

        def g_copy(o):
            t = lax.rem(me + o, ndev)
            d = t // nseq
            return remote(gsend.at[d], gall.at[me], g_s.at[o], g_r.at[me], d, lax.rem(t, nseq))

        def g_arrival(o):
            t = lax.rem(me + ndev - o, ndev)
            d = t // nseq
            return remote(gsend.at[d], gall.at[t], g_s.at[o], g_r.at[t], d, lax.rem(t, nseq))

        def each(count, act, low=1):
            def body(o, c):
                act(o)
                return c
            lax.fori_loop(low, count, body, 0)

        def start_all(count, copy, low=1):
            each(count, lambda o: copy(o).start(), low)

        def finish(count, copy, arrival):
            each(count, lambda o: copy(o).wait_send())
            each(count, lambda o: arrival(o).wait_recv())

        start_all(nz, px_copy)
        xall[me] = xbuf[seq]
        own = pltpu.make_async_copy(pix.at[pl.ds(seq * tf, tf)], pxall.at[seq], wsem.at[2])
        own.start()

        matches = (place_of[...] == marks[...]).astype(F32)
        scale = 2.0 / (4 * values) * jnp.sum(matches, axis=1, keepdims=True)
        h_low, h_high = colv[:, 1:2], colv[:, 2:3]
        w_low, w_high = colv[:, 3:4], colv[:, 4:5]

        def row_shift(v, d):
            m = v.shape[0]
            if d == 0:
                return v
            rolled = pltpu.roll(v, 1 if d < 0 else m - 1, axis=0)
            return rolled * (h_low if d < 0 else h_high)[:m]

        def col_shift(v, d):
            m = v.shape[0]
            if d == 0:
                return v
            rolled = pltpu.roll(v, rows if d < 0 else m - rows, axis=0)
            return rolled * (w_low if d < 0 else w_high)[:m]

        def place(field, frame, v, count):
            for d in (-1, 0, 1):
                field[d + 1, frame:frame + count, 1:cols + 1] = (
                    row_shift(v, d).astype(BF16).reshape(count, cols, rows, v.shape[1]))

        def edges(field):
            zero = jnp.zeros((3, tf + 2, 1, rows, field.shape[4]), BF16)
            field[:, :, 0:1] = zero
            field[:, :, cols + 1:cols + 2] = zero

        first = jnp.where(seq > 0, 1.0, 0.0).astype(F32)
        final = jnp.where(seq < nseq - 1, 1.0, 0.0).astype(F32)

        edges(tfield)
        edges(hfield)
        place(tfield, 1, flat, tf)
        def taps_first(a):
            for bc in range(9):
                k = a * 9 + bc
                im1[:, k * width:(k + 1) * width] = (
                    tfield[bc // 3, a:a + tf, bc % 3:bc % 3 + cols].reshape(n, width))
            span = slice(a * 9 * width, (a + 1) * 9 * width)
            return jnp.dot(im1[:, span], w1[span], preferred_element_type=F32)

        cp1.wait()
        z = taps_first(1) + b1[...]
        for c in th:
            c.wait()
        place(tfield, 0, ordered(thalo[0]) * first, 1)
        place(tfield, tf + 1, ordered(thalo[1]) * final, 1)
        z = z + taps_first(0) + taps_first(2)
        th_ = jnp.tanh(GELU_ROOT * (z + GELU_CUBE * z * z * z))
        slope = 0.5 * (1.0 + th_) + 0.5 * z * (1.0 - th_ * th_) * GELU_ROOT * (
            1.0 + 3.0 * GELU_CUBE * z * z)
        hid = (0.5 * z * (1.0 + th_)).astype(BF16)
        hsend[...] = hid.reshape(tf, cols, rows, mid)
        hh = halo(hsend.at[0], hsend.at[tf - 1], hhalo, hh_s, hh_r)
        for c in hh:
            c.start()
        hid_f = hid.astype(F32)
        place(hfield, 1, hid_f, tf)

        start_all(nseq, px_copy, nz)

        def taps_second(a):
            for ij in range(4):
                i, j = ij // 2, ij % 2
                for bc in range(9):
                    k = a * 9 + bc
                    dh, dw = floor_half(i + bc // 3 - 1), floor_half(j + bc % 3 - 1)
                    im2[ij * n:(ij + 1) * n, k * mid:(k + 1) * mid] = (
                        hfield[dh + 1, a:a + tf, dw + 1:dw + 1 + cols].reshape(n, mid))
            span = slice(a * 9 * mid, (a + 1) * 9 * mid)
            return jnp.dot(im2[:, span], w2[span], preferred_element_type=F32)

        cp2.wait()
        predict = taps_second(1) + b2[...].reshape(1, values)
        for c in hh:
            c.wait()
        start_all(half, x_copy)
        before = hhalo[0].reshape(plane, mid).astype(F32) * first
        after = hhalo[1].reshape(plane, mid).astype(F32) * final
        time_line = jnp.concatenate([before, hid_f, after], axis=0)
        for a in range(3):
            htsend[a * mid:(a + 1) * mid] = (
                time_line[a * plane:a * plane + n].T.astype(BF16))
        each(ndp, lambda o: c_pair(o)[1].start())
        htall[dp] = htsend[...]
        place(hfield, 0, before, 1)
        place(hfield, tf + 1, after, 1)
        predict = predict + taps_second(0) + taps_second(2)

        own.wait()
        finish(nseq, px_copy, px_arrival)
        pix_rows = pxall[...].astype(F32).reshape(n, 4 * values).astype(BF16)
        px = jnp.dot(perm[...], pix_rows, preferred_element_type=F32)
        center = px - jnp.mean(px, axis=-1, keepdims=True)
        spread = jnp.mean(center * center, axis=-1, keepdims=True)
        normed = center * lax.rsqrt(spread + 1e-06)
        cots = []
        for ij in range(4):
            cot = (scale * (predict[ij * n:(ij + 1) * n]
                            - normed[:, ij * values:(ij + 1) * values])).astype(BF16).astype(F32)
            cots.append(cot)
            turned = cot.T
            for d in range(ndp):
                csend[d, ij] = turned[d * vblk:(d + 1) * vblk].astype(BF16)
        each(ndp, lambda o: c_pair(o)[0].start())
        call_[dp] = csend[dp]

        def pair_sums(low, high, shift):
            return (high + shift(low, 1), low + high, shift(high, -1) + low)

        def cell_sums(parts, rshift, cshift):
            by_col = [pair_sums(parts[j], parts[2 + j], rshift) for j in range(2)]
            return [s for b in range(3)
                    for s in pair_sums(by_col[0][b], by_col[1][b], cshift)]

        sums = [s.astype(BF16) for s in cell_sums(cots, row_shift, col_shift)]
        backs = []
        for a in range(3):
            total = jnp.zeros((n, mid), F32)
            for bc in range(9):
                k = a * 9 + bc
                total = total + lax.dot_general(
                    sums[bc], w2[k * mid:(k + 1) * mid], NT, preferred_element_type=F32)
            backs.append(total)
        psend[0] = backs[2][n - plane:]
        psend[1] = backs[0][:plane]
        ph = halo(psend.at[1], psend.at[0], phalo, ph_s, ph_r)
        for c in ph:
            c.start()
        for c in ph:
            c.wait()
        from_prev, from_next = phalo[0] * first, phalo[1] * final
        if tf > 1:
            late = jnp.concatenate([from_prev, backs[2][:n - plane]], axis=0)
            early = jnp.concatenate([backs[0][plane:], from_next], axis=0)
        else:
            late, early = from_prev, from_next
        grad_z = ((backs[1] + late + early) * slope).astype(BF16).astype(F32).T
        for d in range(ndp):
            gsend[d] = grad_z[d * cblk:(d + 1) * cblk].astype(BF16)
        start_all(ndev, g_copy)
        start_all(ndev, x_copy, half)
        gall[me] = gsend[dp]

        each(ndp, lambda o: [c.wait_send() for c in c_pair(o)])
        each(ndp, lambda o: [c.wait_recv() for c in c_arrival(o)])

        def lane_row(v, d):
            rolled = pltpu.roll(v, 1 if d < 0 else n - 1, axis=1)
            return rolled * (lanes_n[0:1] if d < 0 else lanes_n[1:2])

        def lane_col(v, d):
            rolled = pltpu.roll(v, rows if d < 0 else n - rows, axis=1)
            return rolled * (lanes_n[2:3] if d < 0 else lanes_n[3:4])

        acc[...] = jnp.zeros_like(acc)

        def one_clip(q, carry):
            parts = [call_[q, ij].astype(F32) for ij in range(4)]
            stack = jnp.concatenate(cell_sums(parts, lane_row, lane_col), axis=0).astype(BF16)
            acc[...] += lax.dot_general(htall[q], stack, NT, preferred_element_type=F32)
            return carry

        lax.fori_loop(0, ndp, one_clip, 0)

        def part(a, s):
            return acc[pl.ds(pl.multiple_of(a * mid + s * mblk, 8), mblk)]

        for s in range(nz):
            for a in range(3):
                qsend[s, a] = part(a, 2 * s + 1 - core).astype(BF16)
        swap = remote(qsend, qrecv, q_s.at[0], q_r.at[0], dp, 2 * chip + 1 - core)
        swap.start()
        swap.wait()
        for s in range(nz):
            for a in range(3):
                rsend[s, a] = (part(a, 2 * s + core) + qrecv[s, a].astype(F32)).astype(BF16)
        start_all(nz, r_copy)
        rall[chip] = rsend[chip]

        finish(ndev, x_copy, x_arrival)
        finish(ndev, g_copy, g_arrival)
        o1[...] = jnp.zeros_like(o1)

        def one_first(q, carry):
            base = q * nseq
            g = jnp.concatenate([gall[base + s].astype(F32) for s in range(nseq)], axis=1)
            x = jnp.concatenate([xall[base + s] for s in range(nseq)], axis=1)
            pieces = []
            by_row = []
            for b in range(3):
                d = b - 1
                if d == 0:
                    by_row.append(g)
                else:
                    m = pltpu.roll(g, d % clip_lanes, axis=1)
                    by_row.append(m * (lanev[0:1] if d > 0 else lanev[1:2]))
            grid = {}
            for b in range(3):
                for c in range(3):
                    d = c - 1
                    v = by_row[b]
                    if d != 0:
                        v = pltpu.roll(v, (d * rows) % clip_lanes, axis=1)
                        v = v * (lanev[2:3] if d > 0 else lanev[3:4])
                    grid[b, c] = v
            for a in range(3):
                for b in range(3):
                    for c in range(3):
                        d = a - 1
                        v = grid[b, c]
                        if d != 0:
                            v = pltpu.roll(v, (d * plane) % clip_lanes, axis=1)
                            v = v * (lanev[4:5] if d > 0 else lanev[5:6])
                        pieces.append(v)
            stack = jnp.concatenate(pieces, axis=0).astype(BF16)
            o1[...] += lax.dot_general(stack, x, NT, preferred_element_type=F32)
            return carry

        lax.fori_loop(0, ndp, one_first, 0)

        finish(nz, r_copy, r_arrival)
        total = rall[0].astype(F32)
        for s in range(1, nz):
            total = total + rall[s].astype(F32)
        for a in range(3):
            for bc in range(9):
                o2[a * 9 + bc] = total[a, :, bc * vblk:(bc + 1) * vblk]

    return kernel


def per_device(tokens, conv_first, bias_first, conv_second, bias_second, pixels, mask_index):
    ndp, nseq = lax.axis_size("dp"), lax.axis_size("seq")
    tf, rows, cols, width = tokens.shape[1:]
    frames = tf * nseq
    mid, values = conv_second.shape[1], conv_second.shape[2]
    n = tf * rows * cols
    hb = rows // nseq
    dims = (ndp, nseq, frames, tf, rows, cols, width, mid, values)
    plane = rows * cols
    dblk, cblk, vblk, mblk = width // nseq, mid // ndp, values // ndp, mid // nseq
    ndev = ndp * nseq

    idx = np.arange(n, dtype=np.int32)
    t_of, w_of, h_of = idx // plane, idx // rows % cols, idx % rows
    source = (h_of // hb) * (tf * hb * cols) + t_of * (hb * cols) + (h_of % hb) * cols + w_of
    perm = jnp.asarray(source[:, None] == idx[None, :], BF16)
    flat_place = (h_of * cols + w_of)[:plane]
    tperm = jnp.asarray(flat_place[:, None] == idx[None, :plane], BF16)
    place_of = jnp.asarray((h_of * cols + w_of)[:, None])
    colv = jnp.asarray(np.stack([h_of < 0, h_of > 0, h_of < rows - 1,
                                 w_of > 0, w_of < cols - 1], axis=1), F32)
    lanes_n = jnp.asarray(np.stack([h_of > 0, h_of < rows - 1, w_of > 0, w_of < cols - 1]), F32)
    lid = np.arange(frames * plane, dtype=np.int32)
    tl, wl, hl = lid // plane, lid // rows % cols, lid % rows
    lanev = jnp.asarray(np.stack([hl > 0, hl < rows - 1, wl > 0, wl < cols - 1,
                                  tl > 0, tl < frames - 1]), F32)

    vm = pl.BlockSpec(memory_space=pltpu.VMEM)
    hbm = pl.BlockSpec(memory_space=pl.ANY)

    def dma(k):
        return pltpu.SemaphoreType.DMA((k,))

    scratch = [
        pltpu.VMEM((27 * width, mid), BF16),
        pltpu.VMEM((27 * mid, values), BF16),
        pltpu.VMEM((nseq, dblk, n), BF16),
        pltpu.VMEM((ndev, dblk, n), BF16),
        pltpu.VMEM((2, rows, cols, width), BF16),
        pltpu.VMEM((nseq, tf, hb, cols, 4 * values), BF16),
        pltpu.VMEM((3, tf + 2, cols + 2, rows, width), BF16),
        pltpu.VMEM((n, 27 * width), BF16),
        pltpu.VMEM((tf, cols, rows, mid), BF16),
        pltpu.VMEM((2, cols, rows, mid), BF16),
        pltpu.VMEM((3, tf + 2, cols + 2, rows, mid), BF16),
        pltpu.VMEM((4 * n, 27 * mid), BF16),
        pltpu.VMEM((2, plane, mid), F32),
        pltpu.VMEM((2, plane, mid), F32),
        pltpu.VMEM((ndp, 4, vblk, n), BF16),
        pltpu.VMEM((ndp, 4, vblk, n), BF16),
        pltpu.VMEM((3 * mid, n), BF16),
        pltpu.VMEM((ndp, 3 * mid, n), BF16),
        pltpu.VMEM((nseq // 2, 3, mblk, 9 * vblk), BF16),
        pltpu.VMEM((nseq // 2, 3, mblk, 9 * vblk), BF16),
        pltpu.VMEM((nseq // 2, 3, mblk, 9 * vblk), BF16),
        pltpu.VMEM((nseq // 2, 3, mblk, 9 * vblk), BF16),
        pltpu.VMEM((ndp, cblk, n), BF16),
        pltpu.VMEM((ndev, cblk, n), BF16),
        pltpu.VMEM((3 * mid, 9 * vblk), F32),
        dma(3), dma(2), dma(2), dma(nseq), dma(nseq), dma(ndev), dma(ndev),
        dma(2), dma(2), dma(2), dma(2), dma(ndp), dma(ndp), dma(ndp), dma(ndp),
        dma(1), dma(1), dma(nseq // 2), dma(nseq // 2), dma(ndev), dma(ndev),
    ]
    first, second = pl.pallas_call(
        make_kernel(dims),
        out_shape=(jax.ShapeDtypeStruct((27 * cblk, dblk), F32),
                   jax.ShapeDtypeStruct((27, mblk, vblk), F32)),
        in_specs=[vm, hbm, vm, hbm, vm, hbm, vm, vm, vm, vm, vm, vm, vm],
        out_specs=(vm, vm),
        scratch_shapes=scratch,
        compiler_params=pltpu.CompilerParams(
            collective_id=0, has_side_effects=True, vmem_limit_bytes=60 * 1024 * 1024),
        name="step",
    )(tokens[0], conv_first.reshape(27 * width, mid), bias_first.reshape(1, mid),
      conv_second.reshape(27 * mid, values), bias_second,
      pixels[0], mask_index, place_of, tperm, perm, colv, lanev, lanes_n)
    first = first.reshape(27, cblk, dblk).transpose(0, 2, 1)
    return (first, second)


def solution(mesh):
    return jax.shard_map(
        per_device,
        mesh=mesh,
        in_specs=(
            P("dp", "seq", None, None, None),
            P(),
            P(),
            P(),
            P(),
            P("dp", None, "seq", None, None),
            P("dp", None),
        ),
        out_specs=(P(None, "seq", "dp"), P(None, "seq", "dp")),
        check_vma=False,
    )
```

```python
import jax
import jax.numpy as jnp
import numpy as np
from jax import lax
from jax.experimental import pallas as pl
from jax.experimental.pallas import tpu as pltpu
from jax.sharding import PartitionSpec as P

F32 = jnp.float32
BF16 = jnp.bfloat16
NT = (((1,), (1,)), ((), ()))
GELU_ROOT = 0.7978845608028654
GELU_CUBE = 0.044715


def floor_half(v):
    return v // 2 if v >= 0 else -1


def make_kernel(dims):
    ndp, nseq, frames, tf, rows, cols, width, mid, values = dims
    n = tf * cols * rows
    plane = cols * rows
    dblk = width // nseq
    cblk = mid // ndp
    vblk = values // ndp
    mblk = mid // nseq
    ndev = ndp * nseq
    nz = nseq // 2
    quarter = ndev // 4
    clip_lanes = nseq * n

    def kernel(tok, w1_hbm, b1, w2_hbm, b2, pix, marks, place_of, tperm, perm, colv, lanev,
               lanes_n, o1, o2,
               w1, w2, xbuf, xall, thalo, pxall, tfield, im1, hsend, hhalo, hfield, im2,
               psend, phalo, csend, call_, htsend, htall, qsend, qrecv, rsend, rall, gsend, gall, acc,
               wsem, th_s, th_r, px_s, px_r, x_s, x_r, hh_s, hh_r, ph_s, ph_r,
               c_s, c_r, ht_s, ht_r, q_s, q_r, r_s, r_r, g_s, g_r):
        dp = lax.axis_index("dp")
        seq = lax.axis_index("seq")
        me = dp * nseq + seq
        chip, core = seq // 2, lax.rem(seq, 2)
        nxt = lax.rem(seq + 1, nseq)
        prv = lax.rem(seq + nseq - 1, nseq)

        def remote(src, dst, ss, rs, d, s):
            return pltpu.make_async_remote_copy(
                src_ref=src, dst_ref=dst, send_sem=ss, recv_sem=rs,
                device_id=(d, s), device_id_type=pl.DeviceIdType.MESH)

        cp1 = pltpu.make_async_copy(w1_hbm, w1, wsem.at[0])
        cp2 = pltpu.make_async_copy(w2_hbm, w2, wsem.at[1])
        cp1.start()
        cp2.start()

        barrier = pltpu.get_barrier_semaphore()

        def greet(o, c):
            t = lax.rem(me + o, ndev)
            pl.semaphore_signal(barrier, inc=1, device_id=(t // nseq, lax.rem(t, nseq)),
                                device_id_type=pl.DeviceIdType.MESH)
            return c

        lax.fori_loop(1, ndev, greet, 0)

        def ordered(frame):
            raw = frame.astype(F32).reshape(plane, width).astype(BF16)
            return jnp.dot(tperm[...], raw, preferred_element_type=F32)

        flat = jnp.concatenate([ordered(tok[t]) for t in range(tf)], axis=0)
        xt = flat.T
        for s in range(nseq):
            xbuf[s] = xt[s * dblk:(s + 1) * dblk].astype(BF16)
        pl.semaphore_wait(barrier, ndev - 1)

        def halo(first, last, dst, ss, rs):
            return (remote(last, dst.at[0], ss.at[0], rs.at[0], dp, nxt),
                    remote(first, dst.at[1], ss.at[1], rs.at[1], dp, prv))

        th = halo(tok.at[0], tok.at[tf - 1], thalo, th_s, th_r)
        for c in th:
            c.start()

        def px_copy(o):
            s = lax.rem(seq + o, nseq)
            return remote(pix.at[pl.ds(s * tf, tf)], pxall.at[seq], px_s.at[o], px_r.at[seq],
                          dp, s)

        def px_arrival(o):
            s = lax.rem(seq + nseq - o, nseq)
            return remote(pix.at[pl.ds(s * tf, tf)], pxall.at[s], px_s.at[o], px_r.at[s], dp, s)

        def x_copy(o):
            t = lax.rem(me + o, ndev)
            s = lax.rem(t, nseq)
            return remote(xbuf.at[s], xall.at[me], x_s.at[o], x_r.at[me], t // nseq, s)

        def x_arrival(o):
            t = lax.rem(me + ndev - o, ndev)
            s = lax.rem(t, nseq)
            return remote(xbuf.at[s], xall.at[t], x_s.at[o], x_r.at[t], t // nseq, s)

        def c_pair(o):
            d = lax.rem(dp + o, ndp)
            return (remote(csend.at[d], call_.at[dp], c_s.at[o], c_r.at[dp], d, seq),
                    remote(htsend, htall.at[dp], ht_s.at[o], ht_r.at[dp], d, seq))

        def c_arrival(o):
            d = lax.rem(dp + ndp - o, ndp)
            return (remote(csend.at[d], call_.at[d], c_s.at[o], c_r.at[d], d, seq),
                    remote(htsend, htall.at[d], ht_s.at[o], ht_r.at[d], d, seq))

        def r_copy(o):
            s = lax.rem(chip + o, nz)
            return remote(rsend.at[s], rall.at[chip], r_s.at[o], r_r.at[chip], dp,
                          s * 2 + core)

        def r_arrival(o):
            s = lax.rem(chip + nz - o, nz)
            return remote(rsend.at[s], rall.at[s], r_s.at[o], r_r.at[s], dp, s * 2 + core)

        def g_copy(o):
            t = lax.rem(me + o, ndev)
            d = t // nseq
            return remote(gsend.at[d], gall.at[me], g_s.at[o], g_r.at[me], d, lax.rem(t, nseq))

        def g_arrival(o):
            t = lax.rem(me + ndev - o, ndev)
            d = t // nseq
            return remote(gsend.at[d], gall.at[t], g_s.at[o], g_r.at[t], d, lax.rem(t, nseq))

        def each(count, act, low=1):
            def body(o, c):
                act(o)
                return c
            lax.fori_loop(low, count, body, 0)

        def start_all(count, copy, low=1):
            each(count, lambda o: copy(o).start(), low)

        def finish(count, copy, arrival):
            each(count, lambda o: copy(o).wait_send())
            each(count, lambda o: arrival(o).wait_recv())

        start_all(nz, px_copy)
        start_all(quarter, x_copy)
        xall[me] = xbuf[seq]
        own = pltpu.make_async_copy(pix.at[pl.ds(seq * tf, tf)], pxall.at[seq], wsem.at[2])
        own.start()

        matches = (place_of[...] == marks[...]).astype(F32)
        scale = 2.0 / (4 * values) * jnp.sum(matches, axis=1, keepdims=True)
        h_low, h_high = colv[:, 1:2], colv[:, 2:3]
        w_low, w_high = colv[:, 3:4], colv[:, 4:5]

        def row_shift(v, d):
            m = v.shape[0]
            if d == 0:
                return v
            rolled = pltpu.roll(v, 1 if d < 0 else m - 1, axis=0)
            return rolled * (h_low if d < 0 else h_high)[:m]

        def col_shift(v, d):
            m = v.shape[0]
            if d == 0:
                return v
            rolled = pltpu.roll(v, rows if d < 0 else m - rows, axis=0)
            return rolled * (w_low if d < 0 else w_high)[:m]

        def place(field, frame, v, count):
            for d in (-1, 0, 1):
                field[d + 1, frame:frame + count, 1:cols + 1] = (
                    row_shift(v, d).astype(BF16).reshape(count, cols, rows, v.shape[1]))

        def edges(field):
            zero = jnp.zeros((3, tf + 2, 1, rows, field.shape[4]), BF16)
            field[:, :, 0:1] = zero
            field[:, :, cols + 1:cols + 2] = zero

        first = jnp.where(seq > 0, 1.0, 0.0).astype(F32)
        final = jnp.where(seq < nseq - 1, 1.0, 0.0).astype(F32)

        edges(tfield)
        edges(hfield)
        place(tfield, 1, flat, tf)
        def taps_first(a):
            for bc in range(9):
                k = a * 9 + bc
                im1[:, k * width:(k + 1) * width] = (
                    tfield[bc // 3, a:a + tf, bc % 3:bc % 3 + cols].reshape(n, width))
            span = slice(a * 9 * width, (a + 1) * 9 * width)
            return jnp.dot(im1[:, span], w1[span], preferred_element_type=F32)

        cp1.wait()
        z = taps_first(1) + b1[...]
        for c in th:
            c.wait()
        place(tfield, 0, ordered(thalo[0]) * first, 1)
        place(tfield, tf + 1, ordered(thalo[1]) * final, 1)
        z = z + taps_first(0) + taps_first(2)
        th_ = jnp.tanh(GELU_ROOT * (z + GELU_CUBE * z * z * z))
        slope = 0.5 * (1.0 + th_) + 0.5 * z * (1.0 - th_ * th_) * GELU_ROOT * (
            1.0 + 3.0 * GELU_CUBE * z * z)
        hid = (0.5 * z * (1.0 + th_)).astype(BF16)
        hsend[...] = hid.reshape(tf, cols, rows, mid)
        hh = halo(hsend.at[0], hsend.at[tf - 1], hhalo, hh_s, hh_r)
        for c in hh:
            c.start()
        hid_f = hid.astype(F32)
        place(hfield, 1, hid_f, tf)

        start_all(nseq, px_copy, nz)

        def taps_second(a):
            for ij in range(4):
                i, j = ij // 2, ij % 2
                for bc in range(9):
                    k = a * 9 + bc
                    dh, dw = floor_half(i + bc // 3 - 1), floor_half(j + bc % 3 - 1)
                    im2[ij * n:(ij + 1) * n, k * mid:(k + 1) * mid] = (
                        hfield[dh + 1, a:a + tf, dw + 1:dw + 1 + cols].reshape(n, mid))
            span = slice(a * 9 * mid, (a + 1) * 9 * mid)
            return jnp.dot(im2[:, span], w2[span], preferred_element_type=F32)

        cp2.wait()
        predict = taps_second(1) + b2[...].reshape(1, values)
        for c in hh:
            c.wait()
        start_all(3 * quarter, x_copy, quarter)
        before = hhalo[0].reshape(plane, mid).astype(F32) * first
        after = hhalo[1].reshape(plane, mid).astype(F32) * final
        time_line = jnp.concatenate([before, hid_f, after], axis=0)
        for a in range(3):
            htsend[a * mid:(a + 1) * mid] = (
                time_line[a * plane:a * plane + n].T.astype(BF16))
        each(ndp, lambda o: c_pair(o)[1].start())
        htall[dp] = htsend[...]
        place(hfield, 0, before, 1)
        place(hfield, tf + 1, after, 1)
        predict = predict + taps_second(0) + taps_second(2)

        own.wait()
        finish(nseq, px_copy, px_arrival)
        pix_rows = pxall[...].astype(F32).reshape(n, 4 * values).astype(BF16)
        px = jnp.dot(perm[...], pix_rows, preferred_element_type=F32)
        center = px - jnp.mean(px, axis=-1, keepdims=True)
        spread = jnp.mean(center * center, axis=-1, keepdims=True)
        normed = center * lax.rsqrt(spread + 1e-06)
        cots = []
        for ij in range(4):
            cot = (scale * (predict[ij * n:(ij + 1) * n]
                            - normed[:, ij * values:(ij + 1) * values])).astype(BF16).astype(F32)
            cots.append(cot)
            turned = cot.T
            for d in range(ndp):
                csend[d, ij] = turned[d * vblk:(d + 1) * vblk].astype(BF16)
        each(ndp, lambda o: c_pair(o)[0].start())
        call_[dp] = csend[dp]

        def pair_sums(low, high, shift):
            return (high + shift(low, 1), low + high, shift(high, -1) + low)

        def cell_sums(parts, rshift, cshift):
            by_col = [pair_sums(parts[j], parts[2 + j], rshift) for j in range(2)]
            return [s for b in range(3)
                    for s in pair_sums(by_col[0][b], by_col[1][b], cshift)]

        sums = [s.astype(BF16) for s in cell_sums(cots, row_shift, col_shift)]
        backs = []
        for a in range(3):
            total = jnp.zeros((n, mid), F32)
            for bc in range(9):
                k = a * 9 + bc
                total = total + lax.dot_general(
                    sums[bc], w2[k * mid:(k + 1) * mid], NT, preferred_element_type=F32)
            backs.append(total)
        psend[0] = backs[2][n - plane:]
        psend[1] = backs[0][:plane]
        ph = halo(psend.at[1], psend.at[0], phalo, ph_s, ph_r)
        for c in ph:
            c.start()
        for c in ph:
            c.wait()
        from_prev, from_next = phalo[0] * first, phalo[1] * final
        if tf > 1:
            late = jnp.concatenate([from_prev, backs[2][:n - plane]], axis=0)
            early = jnp.concatenate([backs[0][plane:], from_next], axis=0)
        else:
            late, early = from_prev, from_next
        grad_z = ((backs[1] + late + early) * slope).astype(BF16).astype(F32).T
        for d in range(ndp):
            gsend[d] = grad_z[d * cblk:(d + 1) * cblk].astype(BF16)
        start_all(ndev, g_copy)
        start_all(ndev, x_copy, 3 * quarter)
        gall[me] = gsend[dp]

        each(ndp, lambda o: [c.wait_send() for c in c_pair(o)])
        each(ndp, lambda o: [c.wait_recv() for c in c_arrival(o)])

        def lane_row(v, d):
            rolled = pltpu.roll(v, 1 if d < 0 else n - 1, axis=1)
            return rolled * (lanes_n[0:1] if d < 0 else lanes_n[1:2])

        def lane_col(v, d):
            rolled = pltpu.roll(v, rows if d < 0 else n - rows, axis=1)
            return rolled * (lanes_n[2:3] if d < 0 else lanes_n[3:4])

        acc[...] = jnp.zeros_like(acc)

        def one_clip(q, carry):
            parts = [call_[q, ij].astype(F32) for ij in range(4)]
            stack = jnp.concatenate(cell_sums(parts, lane_row, lane_col), axis=0).astype(BF16)
            acc[...] += lax.dot_general(htall[q], stack, NT, preferred_element_type=F32)
            return carry

        lax.fori_loop(0, ndp, one_clip, 0)

        def part(a, s):
            return acc[pl.ds(pl.multiple_of(a * mid + s * mblk, 8), mblk)]

        for s in range(nz):
            for a in range(3):
                qsend[s, a] = part(a, 2 * s + 1 - core).astype(BF16)
        swap = remote(qsend, qrecv, q_s.at[0], q_r.at[0], dp, 2 * chip + 1 - core)
        swap.start()
        swap.wait()
        for s in range(nz):
            for a in range(3):
                rsend[s, a] = (part(a, 2 * s + core) + qrecv[s, a].astype(F32)).astype(BF16)
        start_all(nz, r_copy)
        rall[chip] = rsend[chip]

        finish(ndev, x_copy, x_arrival)
        finish(ndev, g_copy, g_arrival)
        o1[...] = jnp.zeros_like(o1)

        def one_first(q, carry):
            base = q * nseq
            g = jnp.concatenate([gall[base + s].astype(F32) for s in range(nseq)], axis=1)
            x = jnp.concatenate([xall[base + s] for s in range(nseq)], axis=1)
            pieces = []
            by_row = []
            for b in range(3):
                d = b - 1
                if d == 0:
                    by_row.append(g)
                else:
                    m = pltpu.roll(g, d % clip_lanes, axis=1)
                    by_row.append(m * (lanev[0:1] if d > 0 else lanev[1:2]))
            grid = {}
            for b in range(3):
                for c in range(3):
                    d = c - 1
                    v = by_row[b]
                    if d != 0:
                        v = pltpu.roll(v, (d * rows) % clip_lanes, axis=1)
                        v = v * (lanev[2:3] if d > 0 else lanev[3:4])
                    grid[b, c] = v
            for a in range(3):
                for b in range(3):
                    for c in range(3):
                        d = a - 1
                        v = grid[b, c]
                        if d != 0:
                            v = pltpu.roll(v, (d * plane) % clip_lanes, axis=1)
                            v = v * (lanev[4:5] if d > 0 else lanev[5:6])
                        pieces.append(v)
            stack = jnp.concatenate(pieces, axis=0).astype(BF16)
            o1[...] += lax.dot_general(stack, x, NT, preferred_element_type=F32)
            return carry

        lax.fori_loop(0, ndp, one_first, 0)

        finish(nz, r_copy, r_arrival)
        total = rall[0].astype(F32)
        for s in range(1, nz):
            total = total + rall[s].astype(F32)
        for a in range(3):
            for bc in range(9):
                o2[a * 9 + bc] = total[a, :, bc * vblk:(bc + 1) * vblk]

    return kernel


def per_device(tokens, conv_first, bias_first, conv_second, bias_second, pixels, mask_index):
    ndp, nseq = lax.axis_size("dp"), lax.axis_size("seq")
    tf, rows, cols, width = tokens.shape[1:]
    frames = tf * nseq
    mid, values = conv_second.shape[1], conv_second.shape[2]
    n = tf * rows * cols
    hb = rows // nseq
    dims = (ndp, nseq, frames, tf, rows, cols, width, mid, values)
    plane = rows * cols
    dblk, cblk, vblk, mblk = width // nseq, mid // ndp, values // ndp, mid // nseq
    ndev = ndp * nseq

    idx = np.arange(n, dtype=np.int32)
    t_of, w_of, h_of = idx // plane, idx // rows % cols, idx % rows
    source = (h_of // hb) * (tf * hb * cols) + t_of * (hb * cols) + (h_of % hb) * cols + w_of
    perm = jnp.asarray(source[:, None] == idx[None, :], BF16)
    flat_place = (h_of * cols + w_of)[:plane]
    tperm = jnp.asarray(flat_place[:, None] == idx[None, :plane], BF16)
    place_of = jnp.asarray((h_of * cols + w_of)[:, None])
    colv = jnp.asarray(np.stack([h_of < 0, h_of > 0, h_of < rows - 1,
                                 w_of > 0, w_of < cols - 1], axis=1), F32)
    lanes_n = jnp.asarray(np.stack([h_of > 0, h_of < rows - 1, w_of > 0, w_of < cols - 1]), F32)
    lid = np.arange(frames * plane, dtype=np.int32)
    tl, wl, hl = lid // plane, lid // rows % cols, lid % rows
    lanev = jnp.asarray(np.stack([hl > 0, hl < rows - 1, wl > 0, wl < cols - 1,
                                  tl > 0, tl < frames - 1]), F32)

    vm = pl.BlockSpec(memory_space=pltpu.VMEM)
    hbm = pl.BlockSpec(memory_space=pl.ANY)

    def dma(k):
        return pltpu.SemaphoreType.DMA((k,))

    scratch = [
        pltpu.VMEM((27 * width, mid), BF16),
        pltpu.VMEM((27 * mid, values), BF16),
        pltpu.VMEM((nseq, dblk, n), BF16),
        pltpu.VMEM((ndev, dblk, n), BF16),
        pltpu.VMEM((2, rows, cols, width), BF16),
        pltpu.VMEM((nseq, tf, hb, cols, 4 * values), BF16),
        pltpu.VMEM((3, tf + 2, cols + 2, rows, width), BF16),
        pltpu.VMEM((n, 27 * width), BF16),
        pltpu.VMEM((tf, cols, rows, mid), BF16),
        pltpu.VMEM((2, cols, rows, mid), BF16),
        pltpu.VMEM((3, tf + 2, cols + 2, rows, mid), BF16),
        pltpu.VMEM((4 * n, 27 * mid), BF16),
        pltpu.VMEM((2, plane, mid), F32),
        pltpu.VMEM((2, plane, mid), F32),
        pltpu.VMEM((ndp, 4, vblk, n), BF16),
        pltpu.VMEM((ndp, 4, vblk, n), BF16),
        pltpu.VMEM((3 * mid, n), BF16),
        pltpu.VMEM((ndp, 3 * mid, n), BF16),
        pltpu.VMEM((nseq // 2, 3, mblk, 9 * vblk), BF16),
        pltpu.VMEM((nseq // 2, 3, mblk, 9 * vblk), BF16),
        pltpu.VMEM((nseq // 2, 3, mblk, 9 * vblk), BF16),
        pltpu.VMEM((nseq // 2, 3, mblk, 9 * vblk), BF16),
        pltpu.VMEM((ndp, cblk, n), BF16),
        pltpu.VMEM((ndev, cblk, n), BF16),
        pltpu.VMEM((3 * mid, 9 * vblk), F32),
        dma(3), dma(2), dma(2), dma(nseq), dma(nseq), dma(ndev), dma(ndev),
        dma(2), dma(2), dma(2), dma(2), dma(ndp), dma(ndp), dma(ndp), dma(ndp),
        dma(1), dma(1), dma(nseq // 2), dma(nseq // 2), dma(ndev), dma(ndev),
    ]
    first, second = pl.pallas_call(
        make_kernel(dims),
        out_shape=(jax.ShapeDtypeStruct((27 * cblk, dblk), F32),
                   jax.ShapeDtypeStruct((27, mblk, vblk), F32)),
        in_specs=[vm, hbm, vm, hbm, vm, hbm, vm, vm, vm, vm, vm, vm, vm],
        out_specs=(vm, vm),
        scratch_shapes=scratch,
        compiler_params=pltpu.CompilerParams(
            collective_id=0, has_side_effects=True, vmem_limit_bytes=60 * 1024 * 1024),
        name="step",
    )(tokens[0], conv_first.reshape(27 * width, mid), bias_first.reshape(1, mid),
      conv_second.reshape(27 * mid, values), bias_second,
      pixels[0], mask_index, place_of, tperm, perm, colv, lanev, lanes_n)
    first = first.reshape(27, cblk, dblk).transpose(0, 2, 1)
    return (first, second)


def solution(mesh):
    return jax.shard_map(
        per_device,
        mesh=mesh,
        in_specs=(
            P("dp", "seq", None, None, None),
            P(),
            P(),
            P(),
            P(),
            P("dp", None, "seq", None, None),
            P("dp", None),
        ),
        out_specs=(P(None, "seq", "dp"), P(None, "seq", "dp")),
        check_vma=False,
    )
```
